32 devices in a mesh: fsdp: 8 (over z, core), ctx: 2 (over y), tp: 2 (over x).
Axes of the slice: x: 2, y: 2, z: 4, core: 2. Of those that a mesh axis runs over, the one named last changes fastest.
Arguments:
- inputs: bfloat16 [8, 1056, 1024], P('fsdp', 'ctx'), may hold values from -6 to 6
- lengths: int32 [8, 2], P('fsdp'), may hold values from 1 to 528, 1025 in all within a row
- first_gain: bfloat16 [1024], P('fsdp'), may hold values from 0.25 to 1.75
- first_shift: bfloat16 [1024], P('fsdp'), may hold values from -3 to 3
- qkv_weight: bfloat16 [1024, 3, 1024], P('fsdp', None, 'tp'), may hold values from -8 to 8
- qkv_bias: bfloat16 [2, 16, 64], P(None, 'tp', 'fsdp'), may hold values from -3 to 3
- proj_weight: bfloat16 [1024, 1024], P('tp', 'fsdp'), may hold values from -1.5 to 1.5
- proj_bias: bfloat16 [1024], P('fsdp'), may hold values from -3 to 3
- attn_scale: bfloat16 [1024], P('fsdp'), may hold values from 0.5 to 1.5
- second_gain: bfloat16 [1024], P('fsdp'), may hold values from 0.25 to 1.75
- second_shift: bfloat16 [1024], P('fsdp'), may hold values from -3 to 3
- up_weight: bfloat16 [1024, 4096], P('fsdp', 'tp'), may hold values from -0.1875 to 0.1875
- up_bias: bfloat16 [64, 64], P('tp', 'fsdp'), may hold values from -3 to 3
- down_weight: bfloat16 [4096, 1024], P('tp', 'fsdp'), may hold values from -0.09375 to 0.09375
- down_bias: bfloat16 [1024], P('fsdp'), may hold values from -3 to 3
- mlp_scale: bfloat16 [1024], P('fsdp'), may hold values from 0.5 to 1.5
- cotangent: float32 [8, 1056, 1024], P('fsdp', 'ctx'), may hold values from -6 to 6
Outputs:
- output: bfloat16 [8, 1056, 1024], P('fsdp', 'ctx')
- input_grad: bfloat16 [8, 1056, 1024], P('fsdp', 'ctx')
- first_gain_grad: float32 [1024], P('fsdp')
- first_shift_grad: float32 [1024], P('fsdp')
- qkv_weight_grad: float32 [1024, 3, 1024], P('fsdp', None, 'tp')
- qkv_bias_grad: float32 [2, 16, 64], P(None, 'tp', 'fsdp')
- proj_weight_grad: float32 [1024, 1024], P('tp', 'fsdp')
- proj_bias_grad: float32 [1024], P('fsdp')
- attn_scale_grad: float32 [1024], P('fsdp')
- second_gain_grad: float32 [1024], P('fsdp')
- second_shift_grad: float32 [1024], P('fsdp')
- up_weight_grad: float32 [1024, 4096], P('fsdp', 'tp')
- up_bias_grad: float32 [64, 64], P('tp', 'fsdp')
- down_weight_grad: float32 [4096, 1024], P('tp', 'fsdp')
- down_bias_grad: float32 [1024], P('fsdp')
- mlp_scale_grad: float32 [1024], P('fsdp')
The draws below stay inside these ranges and needn't reach their ends.
Inputs may be any that keep to these rules, and one draw needn't show every extreme that they name: Block i of image n holds live tokens in its first lengths[n, i] of 528 slots; each image's lengths sum to 1025.
All inputs are finite; a program needn't handle non-finite values.
Results may differ from the reference program's by a relative error of at most 0.02.
Values may be sent and summed in bfloat16 or wider, within the bound.
No kernel may reach another device: no remote copies, remote signals or barrier semaphores. Data moves between devices by JAX's collectives and lax.ppermute only.
A program may use at most 192 MiB of HBM per device.

```python
import math
import jax
import jax.numpy as jnp
import numpy as np
from jax import lax

D = 1024
H = 16
HD = 64
FF = 4096
SEQ = 1025
IMAGES = 8
BLOCKS = 2
BLK = 528
SLOTS = 1056


def draw_qkv_weight(key, part):
    base_key = jax.random.fold_in(key, 71)
    first_key = jax.random.fold_in(base_key, 0)
    base = jnp.clip(jax.random.normal(first_key, (D, 3, D), jnp.float32), -6.0, 6.0) * D ** (-0.5)
    return base.astype(jnp.bfloat16)


def shard_levels(stream_key, shape, cuts, least, largest):
    loudness = 1.0
    for dim, parts in cuts:
        steps = jax.random.uniform(jax.random.fold_in(jax.random.fold_in(stream_key, 6), dim), (parts,), jnp.float32, least / len(cuts), largest / len(cuts))
        loudness = loudness * jnp.repeat(jnp.exp(steps), shape[dim] // parts).reshape((-1,) + (1,) * (len(shape) - 1 - dim))
    return loudness


def split_up(count, total, bound, lean):
    loads = [(1 << 20) // math.isqrt(grade ** lean) + 1 for grade in range(2, count + 1)]
    surplus, holding = total - bound - (count - 1), [1] * (count - 1)
    while surplus > 0:
        free = [i for i in range(count - 1) if holding[i] < bound]
        mass, remaining = sum([loads[i] for i in free]), surplus
        for i in free:
            extra = min(bound - holding[i], max(1, remaining * loads[i] // mass), surplus)
            holding[i] = holding[i] + extra
            surplus = surplus - extra
    return np.array([bound] + holding)


def ragged_sizes(rng, count, total, reach, lean):
    if count == 2:
        one = jax.random.randint(rng, (), max(1, total - reach), min(reach, total - 1) + 1)
        return jnp.stack([one, total - one])
    sizes = jnp.asarray(split_up(count, total, reach, lean), jnp.int32)
    pairs = (count - 1) // 2
    donor, sink = sizes[1:1 + 2 * pairs:2], sizes[2:2 + 2 * pairs:2]
    margin = jnp.minimum(donor - 1, reach - sink)
    shifted = jax.random.randint(jax.random.fold_in(rng, 1), (pairs,), 0, 1 << 20) % (margin + 1)
    sizes = sizes.at[1:1 + 2 * pairs:2].set(donor - shifted).at[2:2 + 2 * pairs:2].set(sink + shifted)
    return sizes[jax.random.permutation(jax.random.fold_in(rng, 2), count)]


def normal_values(key, dims, width, reach, cuts=(), kind=jnp.bfloat16):
    drawn = jax.random.normal(key, dims, jnp.float32) * width
    if len(cuts) > 0:
        drawn = shard_levels(key, dims, cuts, -0.22, 0.18) * drawn
    return jnp.clip(drawn, min=-reach, max=reach).astype(kind)


def setup_inputs(seed: int = 0) -> dict:
    key_of = jax.random.split(jax.random.key(seed), 18)
    inputs = normal_values(key_of[0], (IMAGES, SLOTS, D), 1.0, 6.0, ((0, 8), (1, 2)))
    lengths = jax.vmap(lambda own: ragged_sizes(own, BLOCKS, SEQ, BLK, 1))(jax.random.split(key_of[1], IMAGES)).reshape((IMAGES, BLOCKS)).astype(jnp.int32)
    first_gain = jnp.clip(1.0 + 0.15 * jax.random.normal(key_of[2], (D,), jnp.float32), 0.25, 1.75).astype(jnp.bfloat16)
    first_shift = normal_values(key_of[3], (D,), 0.5, 3.0, ((0, 8),))
    qkv_weight = draw_qkv_weight(jax.random.fold_in(key_of[17], 71), 0)
    qkv_bias = normal_values(key_of[5], (2, H, HD), 0.5, 3.0, ((1, 2), (2, 8)))
    proj_weight = normal_values(key_of[6], (D, D), (D // 64) ** -0.5, 1.5, ((0, 2), (1, 8)))
    proj_bias = normal_values(key_of[7], (D,), 0.5, 3.0, ((0, 8),))
    attn_scale = jnp.clip(0.5 + 1.0 * jax.random.uniform(key_of[8], (D,), jnp.float32) ** shard_levels(key_of[8], (D,), ((0, 8),), -0.2, 0.2), 0.5, 1.5).astype(jnp.bfloat16)
    second_gain = jnp.clip(1.0 + 0.15 * jax.random.normal(key_of[9], (D,), jnp.float32), 0.25, 1.75).astype(jnp.bfloat16)
    second_shift = normal_values(key_of[10], (D,), 0.5, 3.0, ((0, 8),))
    up_weight = normal_values(key_of[11], (D, FF), D ** -0.5, 0.1875, ((0, 8), (1, 2)))
    up_bias = normal_values(key_of[12], (FF // HD, HD), 0.5, 3.0, ((0, 2), (1, 8)))
    down_weight = normal_values(key_of[13], (FF, D), FF ** -0.5, 0.09375, ((0, 2), (1, 8)))
    down_bias = normal_values(key_of[14], (D,), 0.5, 3.0, ((0, 8),))
    mlp_scale = jnp.clip(0.5 + 1.0 * jax.random.uniform(key_of[15], (D,), jnp.float32) ** shard_levels(key_of[15], (D,), ((0, 8),), -0.2, 0.2), 0.5, 1.5).astype(jnp.bfloat16)
    cotangent = normal_values(key_of[16], (IMAGES, SLOTS, D), 1.0, 6.0, ((0, 8), (1, 2)), jnp.float32)
    return {"inputs": inputs, "lengths": lengths, "first_gain": first_gain, "first_shift": first_shift, "qkv_weight": qkv_weight, "qkv_bias": qkv_bias, "proj_weight": proj_weight, "proj_bias": proj_bias, "attn_scale": attn_scale, "second_gain": second_gain, "second_shift": second_shift, "up_weight": up_weight, "up_bias": up_bias, "down_weight": down_weight, "down_bias": down_bias, "mlp_scale": mlp_scale, "cotangent": cotangent}


epsilon = 1e-06
negative = -1e+30

def normalize(values, gain, shift):
    center = values - lax.optimization_barrier(jnp.mean(values, axis=-1, keepdims=True))
    inverse = lax.rsqrt(lax.optimization_barrier(jnp.mean(center * center, axis=-1, keepdims=True)) + epsilon)
    standard = center * inverse
    return (standard * gain + shift, standard, inverse)

def normalize_back(upstream, standard, inverse, gain):
    scaled = upstream * gain
    return inverse * (scaled - lax.optimization_barrier(jnp.mean(scaled, axis=-1, keepdims=True)) - standard * lax.optimization_barrier(jnp.mean(scaled * standard, axis=-1, keepdims=True)))

def gelu_parts(hidden):
    cumulative = 0.5 * (1.0 + jax.scipy.special.erf(hidden * (1.0 / math.sqrt(2.0))))
    density = jnp.exp(-0.5 * hidden * hidden) * (1.0 / math.sqrt(2.0 * math.pi))
    return (cumulative, cumulative + hidden * density)

def key_usable(lengths, slots, slot_count):
    position = jnp.arange(slot_count, dtype=jnp.int32)
    owners = position // slots
    owner_table = owners[:, None] == jnp.arange(lengths.shape[0], dtype=jnp.int32)[None, :]
    row_limit = lax.optimization_barrier(jnp.sum(jnp.where(owner_table, lengths[None, :], 0), axis=1))
    return position % slots < row_limit

def head_forward(queries, key_rows, value_rows, usable):
    scaling = queries.shape[-1] ** (-0.5)
    scores = jnp.dot(queries, key_rows.T, preferred_element_type=jnp.float32) * scaling
    scores = jnp.where(usable[None, :], scores, negative)
    maximum = lax.optimization_barrier(jnp.max(scores, axis=-1, keepdims=True))
    exponent = jnp.exp(scores - maximum)
    summed = lax.optimization_barrier(jnp.sum(exponent, axis=-1, keepdims=True))
    weights = (exponent / summed).astype(jnp.bfloat16)
    result = jnp.dot(weights, value_rows, preferred_element_type=jnp.float32).astype(jnp.bfloat16)
    return (result, (maximum + jnp.log(summed))[:, 0])

def head_backward(queries, key_rows, value_rows, upstream, logsum, usable):
    scaling = queries.shape[-1] ** (-0.5)
    scores = jnp.dot(queries, key_rows.T, preferred_element_type=jnp.float32) * scaling
    scores = jnp.where(usable[None, :], scores, negative)
    probabilities = jnp.exp(scores - logsum[:, None])
    probs_low = probabilities.astype(jnp.bfloat16)
    value_grad = jnp.dot(probs_low.T, upstream, preferred_element_type=jnp.float32).astype(jnp.bfloat16)
    dprobs = jnp.dot(upstream, value_rows.T, preferred_element_type=jnp.float32)
    row_total = lax.optimization_barrier(jnp.sum(probabilities * dprobs, axis=-1, keepdims=True))
    dscores = (probabilities * (dprobs - row_total) * scaling).astype(jnp.bfloat16)
    query_grad = jnp.dot(dscores, key_rows, preferred_element_type=jnp.float32).astype(jnp.bfloat16)
    key_grad = jnp.dot(dscores.T, queries, preferred_element_type=jnp.float32).astype(jnp.bfloat16)
    return (query_grad, key_grad, value_grad)

def reference(inputs, lengths, first_gain, first_shift, qkv_weight, qkv_bias, proj_weight, proj_bias, attn_scale, second_gain, second_shift, up_weight, up_bias, down_weight, down_bias, mlp_scale, cotangent):
    gain_one = first_gain.astype(jnp.float32)
    shift_one = first_shift.astype(jnp.float32)
    gain_two = second_gain.astype(jnp.float32)
    shift_two = second_shift.astype(jnp.float32)
    scale_one = attn_scale.astype(jnp.float32)
    scale_two = mlp_scale.astype(jnp.float32)
    bias_proj = proj_bias.astype(jnp.float32)
    bias_down = down_bias.astype(jnp.float32)
    bias_up = up_bias.reshape(FF).astype(jnp.float32)
    qkv_matrix = qkv_weight.reshape(D, 3 * D)
    bias_pair = qkv_bias.reshape(2, D).astype(jnp.float32)
    bias_rows = jnp.stack([bias_pair[0], jnp.zeros((D,), jnp.float32), bias_pair[1]])

    def split_heads(matrix):
        return matrix.reshape(SLOTS, H, HD).transpose(1, 0, 2)

    def join_heads(stacked):
        return stacked.transpose(1, 0, 2).reshape(SLOTS, D)

    def one_image(totals, element):
        picture, upstream_raw, image_lengths = element
        usable = key_usable(image_lengths, BLK, SLOTS)
        live_rows = usable.astype(jnp.float32)

        def forward_head(item):
            return head_forward(item[0], item[1], item[2], usable)

        def backward_head(item):
            return head_backward(item[0], item[1], item[2], item[3], item[4], usable)
        source = picture.astype(jnp.float32)
        normed_one, unit_one, inverse_one = normalize(source, gain_one, shift_one)
        low_one = normed_one.astype(jnp.bfloat16)
        qkv = jnp.dot(low_one, qkv_matrix, preferred_element_type=jnp.float32).reshape(SLOTS, 3, D) + bias_rows
        qkv_low = qkv.astype(jnp.bfloat16)
        queries = split_heads(qkv_low[:, 0])
        key_rows = split_heads(qkv_low[:, 1])
        value_rows = split_heads(qkv_low[:, 2])
        attended_heads, logsum = lax.map(forward_head, (queries, key_rows, value_rows))
        attended = join_heads(attended_heads)
        projected = jnp.dot(attended, proj_weight, preferred_element_type=jnp.float32) + bias_proj
        resid = source + scale_one * projected
        normed_two, unit_two, inverse_two = normalize(resid, gain_two, shift_two)
        low_two = normed_two.astype(jnp.bfloat16)
        hidden = jnp.dot(low_two, up_weight, preferred_element_type=jnp.float32) + bias_up
        cumulative, derivative = gelu_parts(hidden)
        activated = (hidden * cumulative).astype(jnp.bfloat16)
        mlp_out = jnp.dot(activated, down_weight, preferred_element_type=jnp.float32) + bias_down
        output = (resid + scale_two * mlp_out).astype(jnp.bfloat16)
        upstream = upstream_raw * live_rows[:, None]
        grad_scale_two = lax.optimization_barrier(jnp.sum(upstream * mlp_out, axis=0))
        dmlp = upstream * scale_two
        grad_down_bias = lax.optimization_barrier(jnp.sum(dmlp, axis=0))
        dmlp_low = dmlp.astype(jnp.bfloat16)
        grad_down = jnp.dot(activated.T, dmlp_low, preferred_element_type=jnp.float32)
        dhidden = jnp.dot(dmlp_low, down_weight.T, preferred_element_type=jnp.float32) * derivative
        grad_up_bias = lax.optimization_barrier(jnp.sum(dhidden, axis=0))
        dhidden_low = dhidden.astype(jnp.bfloat16)
        grad_up = jnp.dot(low_two.T, dhidden_low, preferred_element_type=jnp.float32)
        dnorm_two = jnp.dot(dhidden_low, up_weight.T, preferred_element_type=jnp.float32)
        grad_gain_two = lax.optimization_barrier(jnp.sum(dnorm_two * unit_two, axis=0))
        grad_shift_two = lax.optimization_barrier(jnp.sum(dnorm_two, axis=0))
        dresid = upstream + normalize_back(dnorm_two, unit_two, inverse_two, gain_two)
        grad_scale_one = lax.optimization_barrier(jnp.sum(dresid * projected, axis=0))
        dproj = dresid * scale_one
        grad_proj_bias = lax.optimization_barrier(jnp.sum(dproj, axis=0))
        dproj_low = dproj.astype(jnp.bfloat16)
        grad_proj = jnp.dot(attended.T, dproj_low, preferred_element_type=jnp.float32)
        dattended = jnp.dot(dproj_low, proj_weight.T, preferred_element_type=jnp.float32).astype(jnp.bfloat16)
        query_grad, key_grad, value_grad = lax.map(backward_head, (queries, key_rows, value_rows, split_heads(dattended), logsum))
        query_rows = join_heads(query_grad)
        value_back = join_heads(value_grad)
        dqkv = jnp.concatenate([query_rows, join_heads(key_grad), value_back], axis=1)
        grad_qkv = jnp.dot(low_one.T, dqkv, preferred_element_type=jnp.float32).reshape(D, 3, D)
        grad_qkv_bias = jnp.stack([lax.optimization_barrier(jnp.sum(query_rows, axis=0, dtype=jnp.float32)), lax.optimization_barrier(jnp.sum(value_back, axis=0, dtype=jnp.float32))]).reshape(2, H, HD)
        dnorm_one = jnp.dot(dqkv, qkv_matrix.T, preferred_element_type=jnp.float32)
        grad_gain_one = lax.optimization_barrier(jnp.sum(dnorm_one * unit_one, axis=0))
        grad_shift_one = lax.optimization_barrier(jnp.sum(dnorm_one, axis=0))
        dinput = (dresid + normalize_back(dnorm_one, unit_one, inverse_one, gain_one)).astype(jnp.bfloat16)
        gradients = (grad_gain_one, grad_shift_one, grad_qkv, grad_qkv_bias, grad_proj, grad_proj_bias, grad_scale_one, grad_gain_two, grad_shift_two, grad_up, grad_up_bias.reshape(FF // HD, HD), grad_down, grad_down_bias, grad_scale_two)
        return (tuple((first + second for first, second in zip(totals, gradients))), (output, dinput))
    initial = tuple((jnp.zeros(parameter.shape, jnp.float32) for parameter in (first_gain, first_shift, qkv_weight, qkv_bias, proj_weight, proj_bias, attn_scale, second_gain, second_shift, up_weight, up_bias, down_weight, down_bias, mlp_scale)))
    totals, (outputs, input_grad) = lax.scan(one_image, initial, (inputs, cotangent, lengths))
    return (outputs, input_grad, totals[0], totals[1], totals[2], totals[3], totals[4], totals[5], totals[6], totals[7], totals[8], totals[9], totals[10], totals[11], totals[12], totals[13])
```

```python
import math

import jax
import jax.numpy as jnp
from jax import lax
from jax.experimental import pallas as pl
from jax.experimental.pallas import tpu as pltpu
from jax.sharding import PartitionSpec as P

epsilon = 1e-06
negative = -1e30
f32 = jnp.float32
bf16 = jnp.bfloat16


def normalize(values, gain, shift):
    center = values - jnp.mean(values, axis=-1, keepdims=True)
    inverse = lax.rsqrt(jnp.mean(center * center, axis=-1, keepdims=True) + epsilon)
    standard = center * inverse
    return (standard * gain + shift, standard, inverse)


def normalize_back(upstream, standard, inverse, gain):
    scaled = upstream * gain
    return inverse * (
        scaled
        - jnp.mean(scaled, axis=-1, keepdims=True)
        - standard * jnp.mean(scaled * standard, axis=-1, keepdims=True)
    )


def gelu_parts(hidden):
    cumulative = 0.5 * (1.0 + jax.scipy.special.erf(hidden * (1.0 / math.sqrt(2.0))))
    density = jnp.exp(-0.5 * hidden * hidden) * (1.0 / math.sqrt(2.0 * math.pi))
    return (cumulative, cumulative + hidden * density)


def dot(left, right, dims):
    return lax.dot_general(left, right, (dims, ((), ())), preferred_element_type=f32)


def exchange_sum(part, axis):
    if lax.axis_size(axis) == 2:
        other = lax.ppermute(part, axis, [(0, 1), (1, 0)])
        return part.astype(f32) + other.astype(f32)
    return lax.psum(part, axis).astype(f32)


def ring_shift(value, axis, step):
    size = lax.axis_size(axis)
    return lax.ppermute(value, axis, [(i, (i + step) % size) for i in range(size)])


def lane_masks(rows, width, head_size):
    lane = lax.broadcasted_iota(jnp.int32, (rows, width), 1)
    return [
        (lane // head_size == i).astype(f32) for i in range(width // head_size)
    ]


def scores_by_key(keys, query, usable):
    scores = dot(keys, query, ((1,), (1,)))
    return jnp.where(usable, scores, negative)


def forward_kernel(live_ref, query_ref, *rest, head_size, blocks):
    key_refs, value_refs, out_ref = rest[:blocks], rest[blocks : 2 * blocks], rest[-1]
    rows, width = query_ref.shape
    masks = lane_masks(rows, width, head_size)
    query = query_ref[...].astype(f32) * head_size ** (-0.5)
    keys = jnp.concatenate([ref[...] for ref in key_refs], axis=0)
    values = jnp.concatenate([ref[...] for ref in value_refs], axis=0)
    column = lax.broadcasted_iota(jnp.int32, (1, blocks * rows), 1)
    usable = column < 0
    for i in range(blocks):
        usable = usable | ((column >= i * rows) & (column < i * rows + live_ref[i]))
    result = jnp.zeros((rows, width), f32)
    for mask in masks:
        scores = dot((query * mask).astype(bf16), keys, ((1,), (1,)))
        scores = jnp.where(usable, scores, negative)
        maximum = jnp.max(scores, axis=-1, keepdims=True)
        exponent = jnp.exp(scores - maximum)
        summed = jnp.sum(exponent, axis=-1, keepdims=True)
        weights = (exponent * (1.0 / summed)).astype(bf16)
        result = result + dot(weights, values, ((1,), (0,))) * mask
    out_ref[...] = result.astype(bf16)


def backward_kernel(live_ref, query_ref, grad_ref, *rest, head_size, blocks):
    key_refs, value_refs = rest[:blocks], rest[blocks : 2 * blocks]
    query_grad_ref, own_ref = rest[2 * blocks], rest[2 * blocks + 1]
    other_refs = rest[2 * blocks + 2 :]
    rows, width = query_ref.shape
    scaling = head_size ** (-0.5)
    masks = lane_masks(rows, width, head_size)
    query = query_ref[...].astype(f32)
    grads = grad_ref[...].astype(f32)
    key_position = lax.broadcasted_iota(jnp.int32, (rows, 1), 0)
    query_grad = jnp.zeros((rows, width), f32)
    key_grads = [jnp.zeros((rows, width), f32) for _ in range(blocks)]
    value_grads = [jnp.zeros((rows, width), f32) for _ in range(blocks)]
    for mask in masks:
        head_query = (query * mask).astype(bf16)
        scaled_query = (query * (mask * scaling)).astype(bf16)
        head_grads = (grads * mask).astype(bf16)
        scores = [
            scores_by_key(key_refs[i][...], scaled_query, key_position < live_ref[i])
            for i in range(blocks)
        ]
        maximum = scores[0].max(axis=0, keepdims=True)
        for item in scores[1:]:
            maximum = jnp.maximum(maximum, item.max(axis=0, keepdims=True))
        exponents = [jnp.exp(item - maximum) for item in scores]
        summed = sum(item.sum(axis=0, keepdims=True) for item in exponents)
        share = 1.0 / summed
        probabilities = [item * share for item in exponents]
        dprobs = [dot(value_refs[i][...], head_grads, ((1,), (1,))) for i in range(blocks)]
        row_total = sum(
            (p * d).sum(axis=0, keepdims=True) for p, d in zip(probabilities, dprobs)
        )
        for i in range(blocks):
            value_grads[i] = value_grads[i] + dot(
                probabilities[i].astype(bf16), head_grads, ((1,), (0,))
            )
            dscores = (probabilities[i] * (dprobs[i] - row_total) * scaling).astype(bf16)
            key_grads[i] = key_grads[i] + dot(dscores, head_query, ((1,), (0,)))
            query_grad = query_grad + dot(dscores, key_refs[i][...], ((0,), (0,))) * mask
    query_grad_ref[...] = query_grad.astype(bf16)
    own_ref[0] = key_grads[0]
    own_ref[1] = value_grads[0]
    for i, ref in enumerate(other_refs):
        ref[0] = key_grads[i + 1].astype(bf16)
        ref[1] = value_grads[i + 1].astype(bf16)


def column_block(rows, width, first):
    return pl.BlockSpec((rows, width), lambda p: (0, first + p))


def attend(live, query, own, others, head_size, interpret=False):
    rows, local = query.shape
    width = 2 * head_size
    pairs = local // width
    sources = [own] + list(others)
    blocks = len(sources)
    return pl.pallas_call(
        lambda *refs: forward_kernel(*refs, head_size=head_size, blocks=blocks),
        grid=(pairs,),
        in_specs=[pl.BlockSpec(memory_space=pltpu.SMEM), column_block(rows, width, 0)]
        + [column_block(rows, width, 0)] * blocks
        + [column_block(rows, width, pairs)] * blocks,
        out_specs=column_block(rows, width, 0),
        out_shape=jax.ShapeDtypeStruct((rows, local), bf16),
        cost_estimate=pl.CostEstimate(
            flops=4 * rows * rows * blocks * local,
            bytes_accessed=2 * rows * local * (2 + 2 * blocks),
            transcendentals=rows * rows * blocks * local // head_size,
        ),
        compiler_params=pltpu.CompilerParams(vmem_limit_bytes=56 * 1024 * 1024),
        name="attend",
        interpret=interpret,
    )(live, query, *sources, *sources)


def attend_back(live, query, grads, own, others, head_size, interpret=False):
    rows, local = query.shape
    width = 2 * head_size
    pairs = local // width
    sources = [own] + list(others)
    blocks = len(sources)
    stacked = pl.BlockSpec((2, rows, width), lambda p: (0, 0, p))
    return pl.pallas_call(
        lambda *refs: backward_kernel(*refs, head_size=head_size, blocks=blocks),
        grid=(pairs,),
        in_specs=[pl.BlockSpec(memory_space=pltpu.SMEM)]
        + [column_block(rows, width, 0)] * 2
        + [column_block(rows, width, 0)] * blocks
        + [column_block(rows, width, pairs)] * blocks,
        out_specs=[column_block(rows, width, 0)] + [stacked] * blocks,
        out_shape=[
            jax.ShapeDtypeStruct((rows, local), bf16),
            jax.ShapeDtypeStruct((2, rows, local), f32),
        ]
        + [jax.ShapeDtypeStruct((2, rows, local), bf16)] * (blocks - 1),
        cost_estimate=pl.CostEstimate(
            flops=10 * rows * rows * blocks * local,
            bytes_accessed=2 * rows * local * (3 + 6 * blocks),
            transcendentals=rows * rows * blocks * local // head_size,
        ),
        compiler_params=pltpu.CompilerParams(vmem_limit_bytes=56 * 1024 * 1024),
        name="attend_back",
        interpret=interpret,
    )(live, query, grads, *sources, *sources)


def body(
    inputs,
    lengths,
    first_gain,
    first_shift,
    qkv_weight,
    qkv_bias,
    proj_weight,
    proj_bias,
    attn_scale,
    second_gain,
    second_shift,
    up_weight,
    up_bias,
    down_weight,
    down_bias,
    mlp_scale,
    cotangent,
):
    images, slots, features = inputs.shape
    assert images == 1
    shards = lax.axis_size("fsdp")
    groups = lax.axis_size("ctx")
    place = lax.axis_index("ctx")
    width = qkv_weight.shape[2]
    inner = up_weight.shape[1]
    heads = qkv_bias.shape[1]
    head_size = qkv_bias.shape[2] * shards

    small = [
        first_gain,
        first_shift,
        qkv_bias,
        proj_bias,
        attn_scale,
        second_gain,
        second_shift,
        up_bias,
        down_bias,
        mlp_scale,
    ]
    sizes = [math.prod(item.shape) for item in small]
    packed = jnp.concatenate([item.reshape(-1) for item in small])
    gathered = lax.all_gather(packed, "fsdp", axis=0)
    full = []
    offset = 0
    for size in sizes:
        full.append(gathered[:, offset : offset + size].astype(f32))
        offset += size
    gain_one, shift_one, bias_pair, bias_proj, scale_one = full[:5]
    gain_two, shift_two, bias_up, bias_down, scale_two = full[5:]
    gain_one, shift_one, bias_proj, scale_one, gain_two, shift_two, bias_down, scale_two = [
        item.reshape(1, features)
        for item in (
            gain_one, shift_one, bias_proj, scale_one, gain_two, shift_two, bias_down, scale_two
        )
    ]
    bias_pair = (
        bias_pair.reshape(shards, 2, heads, -1).transpose(1, 2, 0, 3).reshape(2, width)
    )
    bias_up = bias_up.reshape(shards, up_bias.shape[0], -1).transpose(1, 0, 2).reshape(1, inner)

    qkv_matrix = lax.all_gather(
        qkv_weight.reshape(qkv_weight.shape[0], 3 * width), "fsdp", axis=0, tiled=True
    )
    proj_back = lax.all_gather(proj_weight.T, "fsdp", axis=0, tiled=True)
    up_full = lax.all_gather(up_weight, "fsdp", axis=0, tiled=True)
    down_back = lax.all_gather(down_weight.T, "fsdp", axis=0, tiled=True)

    source = inputs.reshape(slots, features).astype(f32)
    normed_one, unit_one, inverse_one = normalize(source, gain_one, shift_one)
    low_one = normed_one.astype(bf16)
    bias_kv = jnp.concatenate([jnp.zeros((width,), f32), bias_pair[1]])
    own = (dot(low_one, qkv_matrix[:, width:], ((1,), (0,))) + bias_kv).astype(bf16)
    others = [ring_shift(own, "ctx", step) for step in range(1, groups)]
    queries = (dot(low_one, qkv_matrix[:, :width], ((1,), (0,))) + bias_pair[0]).astype(bf16)
    order = (place - jnp.arange(groups, dtype=jnp.int32)) % groups
    live = jnp.take(lengths[0], order)
    mixed = attend(live, queries, own, others, head_size)

    proj_part = dot(mixed, proj_back, ((1,), (1,))).astype(bf16)
    projected = exchange_sum(proj_part, "tp") + bias_proj
    resid = source + scale_one * projected
    normed_two, unit_two, inverse_two = normalize(resid, gain_two, shift_two)
    low_two = normed_two.astype(bf16)
    hidden = dot(low_two, up_full, ((1,), (0,))) + bias_up
    cumulative, derivative = gelu_parts(hidden)
    activated = (hidden * cumulative).astype(bf16)

    row = lax.broadcasted_iota(jnp.int32, (slots, 1), 0)
    live_rows = (row < live[0]).astype(f32)
    upstream = cotangent.reshape(slots, features) * live_rows
    dmlp = upstream * scale_two
    grad_down_bias = jnp.sum(dmlp, axis=0)
    dmlp_low = dmlp.astype(bf16)
    dhidden = dot(dmlp_low, down_back, ((1,), (0,))) * derivative
    grad_up_bias = jnp.sum(dhidden, axis=0)
    dhidden_low = dhidden.astype(bf16)
    dnorm_part = dot(dhidden_low, up_full, ((1,), (1,))).astype(bf16)
    dnorm_two = exchange_sum(dnorm_part, "tp")
    down_part = dot(activated, down_back, ((1,), (1,))).astype(bf16)
    down_part, dnorm_two = lax.optimization_barrier((down_part, dnorm_two))
    mlp_out = exchange_sum(down_part, "tp") + bias_down
    output = (resid + scale_two * mlp_out).astype(bf16).reshape(images, slots, features)
    grad_scale_two = jnp.sum(upstream * mlp_out, axis=0)

    def reduce_shards(matrix):
        return lax.psum_scatter(matrix.astype(bf16), "fsdp", scatter_dimension=0, tiled=True)

    grad_up = exchange_sum(reduce_shards(dot(low_two, dhidden_low, ((0,), (0,)))), "ctx")
    grad_down = exchange_sum(reduce_shards(dot(dmlp_low, activated, ((0,), (0,)))), "ctx").T

    grad_gain_two = jnp.sum(dnorm_two * unit_two, axis=0)
    grad_shift_two = jnp.sum(dnorm_two, axis=0)
    dresid = upstream + normalize_back(dnorm_two, unit_two, inverse_two, gain_two)
    grad_scale_one = jnp.sum(dresid * projected, axis=0)
    dproj = dresid * scale_one
    grad_proj_bias = jnp.sum(dproj, axis=0)
    dproj_low = dproj.astype(bf16)
    dmixed = dot(dproj_low, proj_back, ((1,), (0,))).astype(bf16)
    grad_proj = exchange_sum(reduce_shards(dot(dproj_low, mixed, ((0,), (0,)))), "ctx").T

    query_grad, own_grad, *sent = attend_back(live, queries, dmixed, own, others, head_size)
    for step, item in enumerate(sent):
        own_grad = own_grad + ring_shift(item, "ctx", -(step + 1)).astype(f32)
    own_low = own_grad.astype(bf16)
    dqkv = jnp.concatenate([query_grad, own_low[0], own_low[1]], axis=1)
    dnorm_local = dot(dqkv, qkv_matrix, ((1,), (1,))).astype(bf16)
    dnorm_one = exchange_sum(dnorm_local, "tp")
    grad_qkv = exchange_sum(reduce_shards(dot(low_one, dqkv, ((0,), (0,)))), "ctx")
    grad_qkv_bias = jnp.stack(
        [jnp.sum(query_grad.astype(f32), axis=0), jnp.sum(own_low[1].astype(f32), axis=0)]
    )
    grad_gain_one = jnp.sum(dnorm_one * unit_one, axis=0)
    grad_shift_one = jnp.sum(dnorm_one, axis=0)
    dinput = (
        (dresid + normalize_back(dnorm_one, unit_one, inverse_one, gain_one))
        .astype(bf16)
        .reshape(images, slots, features)
    )

    pieces = [
        grad_gain_one,
        grad_shift_one,
        grad_qkv_bias.reshape(2, heads, shards, -1).transpose(2, 0, 1, 3),
        grad_proj_bias,
        grad_scale_one,
        grad_gain_two,
        grad_shift_two,
        grad_up_bias.reshape(up_bias.shape[0], shards, -1).transpose(1, 0, 2),
        grad_down_bias,
        grad_scale_two,
    ]
    sent_small = jnp.concatenate([item.reshape(shards, -1) for item in pieces], axis=1)
    got = lax.all_to_all(sent_small.astype(bf16), "fsdp", split_axis=0, concat_axis=0, tiled=True)
    total = exchange_sum(jnp.sum(got.astype(f32), axis=0).astype(bf16), "ctx")
    results = []
    offset = 0
    for item, size in zip(small, sizes):
        results.append(total[offset : offset + size].reshape(item.shape))
        offset += size
    (
        out_gain_one,
        out_shift_one,
        out_qkv_bias,
        out_proj_bias,
        out_scale_one,
        out_gain_two,
        out_shift_two,
        out_up_bias,
        out_down_bias,
        out_scale_two,
    ) = results
    return (
        output,
        dinput,
        out_gain_one,
        out_shift_one,
        grad_qkv.reshape(qkv_weight.shape),
        out_qkv_bias,
        grad_proj,
        out_proj_bias,
        out_scale_one,
        out_gain_two,
        out_shift_two,
        grad_up,
        out_up_bias,
        grad_down,
        out_down_bias,
        out_scale_two,
    )


def solution(mesh):
    rows = P("fsdp", "ctx", None)
    vector = P("fsdp")
    params = (
        vector,
        vector,
        P("fsdp", None, "tp"),
        P(None, "tp", "fsdp"),
        P("tp", "fsdp"),
        vector,
        vector,
        vector,
        vector,
        P("fsdp", "tp"),
        P("tp", "fsdp"),
        P("tp", "fsdp"),
        vector,
        vector,
    )
    return jax.shard_map(
        body,
        mesh=mesh,
        in_specs=(rows, P("fsdp", None)) + params + (rows,),
        out_specs=(rows, rows) + params,
        check_vma=False,
    )
```

```python
import math

import jax
import jax.numpy as jnp
from jax import lax
from jax.experimental import pallas as pl
from jax.experimental.pallas import tpu as pltpu
from jax.sharding import PartitionSpec as P

epsilon = 1e-06
negative = -1e30
f32 = jnp.float32
bf16 = jnp.bfloat16


def normalize(values, gain, shift):
    center = values - jnp.mean(values, axis=-1, keepdims=True)
    inverse = lax.rsqrt(jnp.mean(center * center, axis=-1, keepdims=True) + epsilon)
    standard = center * inverse
    return (standard * gain + shift, standard, inverse)


def normalize_back(upstream, standard, inverse, gain):
    scaled = upstream * gain
    return inverse * (
        scaled
        - jnp.mean(scaled, axis=-1, keepdims=True)
        - standard * jnp.mean(scaled * standard, axis=-1, keepdims=True)
    )


def gelu_parts(hidden):
    cumulative = 0.5 * (1.0 + jax.scipy.special.erf(hidden * (1.0 / math.sqrt(2.0))))
    density = jnp.exp(-0.5 * hidden * hidden) * (1.0 / math.sqrt(2.0 * math.pi))
    return (cumulative, cumulative + hidden * density)


def dot(left, right, dims):
    return lax.dot_general(left, right, (dims, ((), ())), preferred_element_type=f32)


def swap_pair(part, axis):
    if lax.axis_size(axis) == 2:
        return lax.ppermute(part, axis, [(0, 1), (1, 0)])
    return None


def pair_sum(part, other, axis):
    if other is None:
        return lax.psum(part, axis).astype(f32)
    return part.astype(f32) + other.astype(f32)


def exchange_sum(part, axis):
    return pair_sum(part, swap_pair(part, axis), axis)


def after(value, *events):
    if value is None:
        return None
    return lax.optimization_barrier((value,) + events)[0]


def ring_shift(value, axis, step):
    size = lax.axis_size(axis)
    return lax.ppermute(value, axis, [(i, (i + step) % size) for i in range(size)])


def lane_masks(rows, width, head_size):
    lane = lax.broadcasted_iota(jnp.int32, (rows, width), 1)
    return [
        (lane // head_size == i).astype(f32) for i in range(width // head_size)
    ]


def scores_by_key(keys, query, usable):
    scores = dot(keys, query, ((1,), (1,)))
    return jnp.where(usable, scores, negative)


def forward_kernel(live_ref, query_ref, *rest, head_size, blocks):
    key_refs, value_refs, out_ref = rest[:blocks], rest[blocks : 2 * blocks], rest[-1]
    rows, width = query_ref.shape
    masks = lane_masks(rows, width, head_size)
    query = query_ref[...].astype(f32) * head_size ** (-0.5)
    keys = jnp.concatenate([ref[...] for ref in key_refs], axis=0)
    values = jnp.concatenate([ref[...] for ref in value_refs], axis=0)
    column = lax.broadcasted_iota(jnp.int32, (1, blocks * rows), 1)
    usable = column < 0
    for i in range(blocks):
        usable = usable | ((column >= i * rows) & (column < i * rows + live_ref[i]))
    result = jnp.zeros((rows, width), f32)
    for mask in masks:
        scores = dot((query * mask).astype(bf16), keys, ((1,), (1,)))
        scores = jnp.where(usable, scores, negative)
        maximum = jnp.max(scores, axis=-1, keepdims=True)
        exponent = jnp.exp(scores - maximum)
        summed = jnp.sum(exponent, axis=-1, keepdims=True)
        weights = (exponent * (1.0 / summed)).astype(bf16)
        result = result + dot(weights, values, ((1,), (0,))) * mask
    out_ref[...] = result.astype(bf16)


def backward_kernel(live_ref, query_ref, grad_ref, *rest, head_size, blocks):
    key_refs, value_refs = rest[:blocks], rest[blocks : 2 * blocks]
    query_grad_ref, own_ref = rest[2 * blocks], rest[2 * blocks + 1]
    other_refs = rest[2 * blocks + 2 :]
    rows, width = query_ref.shape
    scaling = head_size ** (-0.5)
    masks = lane_masks(rows, width, head_size)
    query = query_ref[...].astype(f32)
    grads = grad_ref[...].astype(f32)
    key_position = lax.broadcasted_iota(jnp.int32, (rows, 1), 0)
    query_grad = jnp.zeros((rows, width), f32)
    key_grads = [jnp.zeros((rows, width), f32) for _ in range(blocks)]
    value_grads = [jnp.zeros((rows, width), f32) for _ in range(blocks)]
    for mask in masks:
        head_query = (query * mask).astype(bf16)
        scaled_query = (query * (mask * scaling)).astype(bf16)
        head_grads = (grads * mask).astype(bf16)
        scores = [
            scores_by_key(key_refs[i][...], scaled_query, key_position < live_ref[i])
            for i in range(blocks)
        ]
        maximum = scores[0].max(axis=0, keepdims=True)
        for item in scores[1:]:
            maximum = jnp.maximum(maximum, item.max(axis=0, keepdims=True))
        exponents = [jnp.exp(item - maximum) for item in scores]
        summed = sum(item.sum(axis=0, keepdims=True) for item in exponents)
        share = 1.0 / summed
        probabilities = [item * share for item in exponents]
        dprobs = [dot(value_refs[i][...], head_grads, ((1,), (1,))) for i in range(blocks)]
        row_total = sum(
            (p * d).sum(axis=0, keepdims=True) for p, d in zip(probabilities, dprobs)
        )
        for i in range(blocks):
            value_grads[i] = value_grads[i] + dot(
                probabilities[i].astype(bf16), head_grads, ((1,), (0,))
            )
            dscores = (probabilities[i] * (dprobs[i] - row_total) * scaling).astype(bf16)
            key_grads[i] = key_grads[i] + dot(dscores, head_query, ((1,), (0,)))
            query_grad = query_grad + dot(dscores, key_refs[i][...], ((0,), (0,))) * mask
    query_grad_ref[...] = query_grad.astype(bf16)
    own_ref[0] = key_grads[0]
    own_ref[1] = value_grads[0]
    for i, ref in enumerate(other_refs):
        ref[0] = key_grads[i + 1].astype(bf16)
        ref[1] = value_grads[i + 1].astype(bf16)


def column_block(rows, width, first):
    return pl.BlockSpec((rows, width), lambda p: (0, first + p))


def attend(live, query, own, others, head_size, interpret=False):
    rows, local = query.shape
    width = 2 * head_size
    pairs = local // width
    sources = [own] + list(others)
    blocks = len(sources)
    return pl.pallas_call(
        lambda *refs: forward_kernel(*refs, head_size=head_size, blocks=blocks),
        grid=(pairs,),
        in_specs=[pl.BlockSpec(memory_space=pltpu.SMEM), column_block(rows, width, 0)]
        + [column_block(rows, width, 0)] * blocks
        + [column_block(rows, width, pairs)] * blocks,
        out_specs=column_block(rows, width, 0),
        out_shape=jax.ShapeDtypeStruct((rows, local), bf16),
        cost_estimate=pl.CostEstimate(
            flops=4 * rows * rows * blocks * local,
            bytes_accessed=2 * rows * local * (2 + 2 * blocks),
            transcendentals=rows * rows * blocks * local // head_size,
        ),
        compiler_params=pltpu.CompilerParams(vmem_limit_bytes=56 * 1024 * 1024),
        name="attend",
        interpret=interpret,
    )(live, query, *sources, *sources)


def attend_back(live, query, grads, own, others, head_size, interpret=False):
    rows, local = query.shape
    width = 2 * head_size
    pairs = local // width
    sources = [own] + list(others)
    blocks = len(sources)
    stacked = pl.BlockSpec((2, rows, width), lambda p: (0, 0, p))
    return pl.pallas_call(
        lambda *refs: backward_kernel(*refs, head_size=head_size, blocks=blocks),
        grid=(pairs,),
        in_specs=[pl.BlockSpec(memory_space=pltpu.SMEM)]
        + [column_block(rows, width, 0)] * 2
        + [column_block(rows, width, 0)] * blocks
        + [column_block(rows, width, pairs)] * blocks,
        out_specs=[column_block(rows, width, 0)] + [stacked] * blocks,
        out_shape=[
            jax.ShapeDtypeStruct((rows, local), bf16),
            jax.ShapeDtypeStruct((2, rows, local), f32),
        ]
        + [jax.ShapeDtypeStruct((2, rows, local), bf16)] * (blocks - 1),
        cost_estimate=pl.CostEstimate(
            flops=10 * rows * rows * blocks * local,
            bytes_accessed=2 * rows * local * (3 + 6 * blocks),
            transcendentals=rows * rows * blocks * local // head_size,
        ),
        compiler_params=pltpu.CompilerParams(vmem_limit_bytes=56 * 1024 * 1024),
        name="attend_back",
        interpret=interpret,
    )(live, query, grads, *sources, *sources)


def body(
    inputs,
    lengths,
    first_gain,
    first_shift,
    qkv_weight,
    qkv_bias,
    proj_weight,
    proj_bias,
    attn_scale,
    second_gain,
    second_shift,
    up_weight,
    up_bias,
    down_weight,
    down_bias,
    mlp_scale,
    cotangent,
):
    images, slots, features = inputs.shape
    assert images == 1
    shards = lax.axis_size("fsdp")
    groups = lax.axis_size("ctx")
    place = lax.axis_index("ctx")
    width = qkv_weight.shape[2]
    inner = up_weight.shape[1]
    heads = qkv_bias.shape[1]
    head_size = qkv_bias.shape[2] * shards

    small = [
        first_gain,
        first_shift,
        qkv_bias,
        proj_bias,
        attn_scale,
        second_gain,
        second_shift,
        up_bias,
        down_bias,
        mlp_scale,
    ]
    sizes = [math.prod(item.shape) for item in small]
    packed = jnp.concatenate([item.reshape(-1) for item in small])
    gathered = lax.all_gather(packed, "fsdp", axis=0)
    full = []
    offset = 0
    for size in sizes:
        full.append(gathered[:, offset : offset + size].astype(f32))
        offset += size
    gain_one, shift_one, bias_pair, bias_proj, scale_one = full[:5]
    gain_two, shift_two, bias_up, bias_down, scale_two = full[5:]
    gain_one, shift_one, bias_proj, scale_one, gain_two, shift_two, bias_down, scale_two = [
        item.reshape(1, features)
        for item in (
            gain_one, shift_one, bias_proj, scale_one, gain_two, shift_two, bias_down, scale_two
        )
    ]
    bias_pair = (
        bias_pair.reshape(shards, 2, heads, -1).transpose(1, 2, 0, 3).reshape(2, width)
    )
    bias_up = bias_up.reshape(shards, up_bias.shape[0], -1).transpose(1, 0, 2).reshape(1, inner)

    attn_part = jnp.concatenate(
        [qkv_weight.reshape(qkv_weight.shape[0], 3 * width), proj_weight.T], axis=1
    )
    attn_full = lax.all_gather(attn_part, "fsdp", axis=0, tiled=True)
    qkv_matrix = attn_full[:, : 3 * width]
    proj_back = attn_full[:, 3 * width :]
    mlp_part = jnp.concatenate([up_weight, down_weight.T], axis=1)
    mlp_full = lax.all_gather(mlp_part, "fsdp", axis=0, tiled=True)
    up_full = mlp_full[:, :inner]
    down_back = mlp_full[:, inner:]

    source = inputs.reshape(slots, features).astype(f32)
    normed_one, unit_one, inverse_one = normalize(source, gain_one, shift_one)
    low_one = normed_one.astype(bf16)
    bias_kv = jnp.concatenate([jnp.zeros((width,), f32), bias_pair[1]])
    own = (dot(low_one, qkv_matrix[:, width:], ((1,), (0,))) + bias_kv).astype(bf16)
    others = [ring_shift(own, "ctx", step) for step in range(1, groups)]
    queries = (dot(low_one, qkv_matrix[:, :width], ((1,), (0,))) + bias_pair[0]).astype(bf16)
    order = (place - jnp.arange(groups, dtype=jnp.int32)) % groups
    live = jnp.take(lengths[0], order)
    mixed = attend(live, queries, own, others, head_size)

    proj_part = dot(mixed, proj_back, ((1,), (1,))).astype(bf16)
    projected = exchange_sum(proj_part, "tp") + bias_proj
    resid = source + scale_one * projected
    normed_two, unit_two, inverse_two = normalize(resid, gain_two, shift_two)
    low_two = normed_two.astype(bf16)
    hidden = dot(low_two, up_full, ((1,), (0,))) + bias_up
    cumulative, derivative = gelu_parts(hidden)
    activated = (hidden * cumulative).astype(bf16)

    row = lax.broadcasted_iota(jnp.int32, (slots, 1), 0)
    live_rows = (row < live[0]).astype(f32)
    upstream = cotangent.reshape(slots, features) * live_rows
    dmlp = upstream * scale_two
    grad_down_bias = jnp.sum(dmlp, axis=0)
    dmlp_low = dmlp.astype(bf16)
    dhidden = dot(dmlp_low, down_back, ((1,), (0,))) * derivative
    grad_up_bias = jnp.sum(dhidden, axis=0)
    dhidden_low = dhidden.astype(bf16)
    dnorm_part = dot(dhidden_low, up_full, ((1,), (1,))).astype(bf16)
    dnorm_other = swap_pair(dnorm_part, "tp")
    up_part = dot(low_two, dhidden_low, ((0,), (0,))).astype(bf16)
    down_grad_part = dot(dmlp_low, activated, ((0,), (0,))).astype(bf16)
    down_part = dot(activated, down_back, ((1,), (1,))).astype(bf16)
    dnorm_other = after(dnorm_other, up_part, down_grad_part, down_part)
    dnorm_two = pair_sum(dnorm_part, dnorm_other, "tp")
    mlp_other = swap_pair(after(down_part, dnorm_two), "tp")

    def reduce_shards(matrix):
        return lax.psum_scatter(matrix, "fsdp", scatter_dimension=0, tiled=True)

    up_shard = reduce_shards(up_part)
    down_shard = reduce_shards(down_grad_part)

    grad_gain_two = jnp.sum(dnorm_two * unit_two, axis=0)
    grad_shift_two = jnp.sum(dnorm_two, axis=0)
    dresid = upstream + normalize_back(dnorm_two, unit_two, inverse_two, gain_two)
    grad_scale_one = jnp.sum(dresid * projected, axis=0)
    dproj = dresid * scale_one
    grad_proj_bias = jnp.sum(dproj, axis=0)
    dproj_low = dproj.astype(bf16)
    dmixed = dot(dproj_low, proj_back, ((1,), (0,))).astype(bf16)
    proj_grad_part = dot(dproj_low, mixed, ((0,), (0,))).astype(bf16)
    proj_shard = reduce_shards(proj_grad_part)

    query_grad, own_grad, *sent = attend_back(live, queries, dmixed, own, others, head_size)
    mlp_other = after(mlp_other, query_grad)
    mlp_out = pair_sum(down_part, mlp_other, "tp") + bias_down
    output = (resid + scale_two * mlp_out).astype(bf16).reshape(images, slots, features)
    grad_scale_two = jnp.sum(upstream * mlp_out, axis=0)
    for step, item in enumerate(sent):
        own_grad = own_grad + ring_shift(item, "ctx", -(step + 1)).astype(f32)
    own_low = own_grad.astype(bf16)
    dqkv = jnp.concatenate([query_grad, own_low[0], own_low[1]], axis=1)
    dnorm_local = dot(dqkv, qkv_matrix, ((1,), (1,))).astype(bf16)
    dnorm_one = exchange_sum(dnorm_local, "tp")
    qkv_part = dot(low_one, dqkv, ((0,), (0,))).astype(bf16)
    qkv_shard = reduce_shards(qkv_part)
    grad_up = exchange_sum(up_shard, "ctx")
    grad_down = exchange_sum(down_shard, "ctx").T
    grad_proj = exchange_sum(proj_shard, "ctx").T
    grad_qkv = exchange_sum(after(qkv_shard, grad_up, grad_down, grad_proj), "ctx")
    grad_qkv_bias = jnp.stack(
        [jnp.sum(query_grad.astype(f32), axis=0), jnp.sum(own_low[1].astype(f32), axis=0)]
    )
    grad_gain_one = jnp.sum(dnorm_one * unit_one, axis=0)
    grad_shift_one = jnp.sum(dnorm_one, axis=0)
    dinput = (
        (dresid + normalize_back(dnorm_one, unit_one, inverse_one, gain_one))
        .astype(bf16)
        .reshape(images, slots, features)
    )

    pieces = [
        grad_gain_one,
        grad_shift_one,
        grad_qkv_bias.reshape(2, heads, shards, -1).transpose(2, 0, 1, 3),
        grad_proj_bias,
        grad_scale_one,
        grad_gain_two,
        grad_shift_two,
        grad_up_bias.reshape(up_bias.shape[0], shards, -1).transpose(1, 0, 2),
        grad_down_bias,
        grad_scale_two,
    ]
    sent_small = jnp.concatenate([item.reshape(shards, -1) for item in pieces], axis=1)
    got = lax.all_to_all(sent_small.astype(bf16), "fsdp", split_axis=0, concat_axis=0, tiled=True)
    total = exchange_sum(jnp.sum(got.astype(f32), axis=0).astype(bf16), "ctx")
    results = []
    offset = 0
    for item, size in zip(small, sizes):
        results.append(total[offset : offset + size].reshape(item.shape))
        offset += size
    (
        out_gain_one,
        out_shift_one,
        out_qkv_bias,
        out_proj_bias,
        out_scale_one,
        out_gain_two,
        out_shift_two,
        out_up_bias,
        out_down_bias,
        out_scale_two,
    ) = results
    return (
        output,
        dinput,
        out_gain_one,
        out_shift_one,
        grad_qkv.reshape(qkv_weight.shape),
        out_qkv_bias,
        grad_proj,
        out_proj_bias,
        out_scale_one,
        out_gain_two,
        out_shift_two,
        grad_up,
        out_up_bias,
        grad_down,
        out_down_bias,
        out_scale_two,
    )


def solution(mesh):
    rows = P("fsdp", "ctx", None)
    vector = P("fsdp")
    params = (
        vector,
        vector,
        P("fsdp", None, "tp"),
        P(None, "tp", "fsdp"),
        P("tp", "fsdp"),
        vector,
        vector,
        vector,
        vector,
        P("fsdp", "tp"),
        P("tp", "fsdp"),
        P("tp", "fsdp"),
        vector,
        vector,
    )

    return jax.shard_map(
        body,
        mesh=mesh,
        in_specs=(rows, P("fsdp", None)) + params + (rows,),
        out_specs=(rows, rows) + params,
        check_vma=False,
    )
```

```python
import math

import jax
import jax.numpy as jnp
from jax import lax
from jax.experimental import pallas as pl
from jax.experimental.pallas import tpu as pltpu
from jax.sharding import PartitionSpec as P

epsilon = 1e-06
negative = -1e30
f32 = jnp.float32
bf16 = jnp.bfloat16


def normalize(values, gain, shift):
    center = values - jnp.mean(values, axis=-1, keepdims=True)
    inverse = lax.rsqrt(jnp.mean(center * center, axis=-1, keepdims=True) + epsilon)
    standard = center * inverse
    return (standard * gain + shift, standard, inverse)


def normalize_back(upstream, standard, inverse, gain):
    scaled = upstream * gain
    return inverse * (
        scaled
        - jnp.mean(scaled, axis=-1, keepdims=True)
        - standard * jnp.mean(scaled * standard, axis=-1, keepdims=True)
    )


def gelu_parts(hidden):
    cumulative = 0.5 * (1.0 + jax.scipy.special.erf(hidden * (1.0 / math.sqrt(2.0))))
    density = jnp.exp(-0.5 * hidden * hidden) * (1.0 / math.sqrt(2.0 * math.pi))
    return (cumulative, cumulative + hidden * density)


def dot(left, right, dims):
    return lax.dot_general(left, right, (dims, ((), ())), preferred_element_type=f32)


def swap_pair(part, axis):
    if lax.axis_size(axis) == 2:
        return lax.ppermute(part, axis, [(0, 1), (1, 0)])
    return None


def pair_sum(part, other, axis):
    if other is None:
        return lax.psum(part, axis).astype(f32)
    return part.astype(f32) + other.astype(f32)


def exchange_sum(part, axis):
    return pair_sum(part, swap_pair(part, axis), axis)


def after(value, *events):
    if value is None:
        return None
    return lax.optimization_barrier((value,) + events)[0]


def ring_shift(value, axis, step):
    size = lax.axis_size(axis)
    return lax.ppermute(value, axis, [(i, (i + step) % size) for i in range(size)])


def lane_masks(rows, width, head_size):
    lane = lax.broadcasted_iota(jnp.int32, (rows, width), 1)
    return [
        (lane // head_size == i).astype(f32) for i in range(width // head_size)
    ]


def scores_by_key(keys, query, usable):
    scores = dot(keys, query, ((1,), (1,)))
    return jnp.where(usable, scores, negative)


def forward_kernel(live_ref, query_ref, *rest, head_size, blocks):
    key_refs, value_refs, out_ref = rest[:blocks], rest[blocks : 2 * blocks], rest[-1]
    rows, width = query_ref.shape
    masks = lane_masks(rows, width, head_size)
    query = query_ref[...].astype(f32) * head_size ** (-0.5)
    keys = jnp.concatenate([ref[...] for ref in key_refs], axis=0)
    values = jnp.concatenate([ref[...] for ref in value_refs], axis=0)
    column = lax.broadcasted_iota(jnp.int32, (1, blocks * rows), 1)
    usable = column < 0
    for i in range(blocks):
        usable = usable | ((column >= i * rows) & (column < i * rows + live_ref[i]))
    result = jnp.zeros((rows, width), f32)
    for mask in masks:
        scores = dot((query * mask).astype(bf16), keys, ((1,), (1,)))
        scores = jnp.where(usable, scores, negative)
        maximum = jnp.max(scores, axis=-1, keepdims=True)
        exponent = jnp.exp(scores - maximum)
        summed = jnp.sum(exponent, axis=-1, keepdims=True)
        weights = (exponent * (1.0 / summed)).astype(bf16)
        result = result + dot(weights, values, ((1,), (0,))) * mask
    out_ref[...] = result.astype(bf16)


def backward_kernel(live_ref, query_ref, grad_ref, *rest, head_size, blocks):
    key_refs, value_refs = rest[:blocks], rest[blocks : 2 * blocks]
    query_grad_ref, own_ref = rest[2 * blocks], rest[2 * blocks + 1]
    other_refs = rest[2 * blocks + 2 :]
    rows, width = query_ref.shape
    scaling = head_size ** (-0.5)
    masks = lane_masks(rows, width, head_size)
    query = query_ref[...].astype(f32)
    grads = grad_ref[...].astype(f32)
    key_position = lax.broadcasted_iota(jnp.int32, (rows, 1), 0)
    query_grad = jnp.zeros((rows, width), f32)
    key_grads = [jnp.zeros((rows, width), f32) for _ in range(blocks)]
    value_grads = [jnp.zeros((rows, width), f32) for _ in range(blocks)]
    for mask in masks:
        head_query = (query * mask).astype(bf16)
        scaled_query = (query * (mask * scaling)).astype(bf16)
        head_grads = (grads * mask).astype(bf16)
        scores = [
            scores_by_key(key_refs[i][...], scaled_query, key_position < live_ref[i])
            for i in range(blocks)
        ]
        maximum = scores[0].max(axis=0, keepdims=True)
        for item in scores[1:]:
            maximum = jnp.maximum(maximum, item.max(axis=0, keepdims=True))
        exponents = [jnp.exp(item - maximum) for item in scores]
        summed = sum(item.sum(axis=0, keepdims=True) for item in exponents)
        share = 1.0 / summed
        probabilities = [item * share for item in exponents]
        dprobs = [dot(value_refs[i][...], head_grads, ((1,), (1,))) for i in range(blocks)]
        row_total = sum(
            (p * d).sum(axis=0, keepdims=True) for p, d in zip(probabilities, dprobs)
        )
        for i in range(blocks):
            value_grads[i] = value_grads[i] + dot(
                probabilities[i].astype(bf16), head_grads, ((1,), (0,))
            )
            dscores = (probabilities[i] * (dprobs[i] - row_total) * scaling).astype(bf16)
            key_grads[i] = key_grads[i] + dot(dscores, head_query, ((1,), (0,)))
            query_grad = query_grad + dot(dscores, key_refs[i][...], ((0,), (0,))) * mask
    query_grad_ref[...] = query_grad.astype(bf16)
    own_ref[0] = key_grads[0]
    own_ref[1] = value_grads[0]
    for i, ref in enumerate(other_refs):
        ref[0] = key_grads[i + 1].astype(bf16)
        ref[1] = value_grads[i + 1].astype(bf16)


def column_block(rows, width, first):
    return pl.BlockSpec((rows, width), lambda p: (0, first + p))


def attend(live, query, own, others, head_size, interpret=False):
    rows, local = query.shape
    width = 2 * head_size
    pairs = local // width
    sources = [own] + list(others)
    blocks = len(sources)
    return pl.pallas_call(
        lambda *refs: forward_kernel(*refs, head_size=head_size, blocks=blocks),
        grid=(pairs,),
        in_specs=[pl.BlockSpec(memory_space=pltpu.SMEM), column_block(rows, width, 0)]
        + [column_block(rows, width, 0)] * blocks
        + [column_block(rows, width, pairs)] * blocks,
        out_specs=column_block(rows, width, 0),
        out_shape=jax.ShapeDtypeStruct((rows, local), bf16),
        cost_estimate=pl.CostEstimate(
            flops=4 * rows * rows * blocks * local,
            bytes_accessed=2 * rows * local * (2 + 2 * blocks),
            transcendentals=rows * rows * blocks * local // head_size,
        ),
        compiler_params=pltpu.CompilerParams(vmem_limit_bytes=56 * 1024 * 1024),
        name="attend",
        interpret=interpret,
    )(live, query, *sources, *sources)


def attend_back(live, query, grads, own, others, head_size, interpret=False):
    rows, local = query.shape
    width = 2 * head_size
    pairs = local // width
    sources = [own] + list(others)
    blocks = len(sources)
    stacked = pl.BlockSpec((2, rows, width), lambda p: (0, 0, p))
    return pl.pallas_call(
        lambda *refs: backward_kernel(*refs, head_size=head_size, blocks=blocks),
        grid=(pairs,),
        in_specs=[pl.BlockSpec(memory_space=pltpu.SMEM)]
        + [column_block(rows, width, 0)] * 2
        + [column_block(rows, width, 0)] * blocks
        + [column_block(rows, width, pairs)] * blocks,
        out_specs=[column_block(rows, width, 0)] + [stacked] * blocks,
        out_shape=[
            jax.ShapeDtypeStruct((rows, local), bf16),
            jax.ShapeDtypeStruct((2, rows, local), f32),
        ]
        + [jax.ShapeDtypeStruct((2, rows, local), bf16)] * (blocks - 1),
        cost_estimate=pl.CostEstimate(
            flops=10 * rows * rows * blocks * local,
            bytes_accessed=2 * rows * local * (3 + 6 * blocks),
            transcendentals=rows * rows * blocks * local // head_size,
        ),
        compiler_params=pltpu.CompilerParams(vmem_limit_bytes=56 * 1024 * 1024),
        name="attend_back",
        interpret=interpret,
    )(live, query, grads, *sources, *sources)


def body(
    inputs,
    lengths,
    first_gain,
    first_shift,
    qkv_weight,
    qkv_bias,
    proj_weight,
    proj_bias,
    attn_scale,
    second_gain,
    second_shift,
    up_weight,
    up_bias,
    down_weight,
    down_bias,
    mlp_scale,
    cotangent,
):
    images, slots, features = inputs.shape
    assert images == 1
    shards = lax.axis_size("fsdp")
    groups = lax.axis_size("ctx")
    place = lax.axis_index("ctx")
    width = qkv_weight.shape[2]
    inner = up_weight.shape[1]
    heads = qkv_bias.shape[1]
    head_size = qkv_bias.shape[2] * shards

    small = [
        first_gain,
        first_shift,
        qkv_bias,
        proj_bias,
        attn_scale,
        second_gain,
        second_shift,
        up_bias,
        down_bias,
        mlp_scale,
    ]
    sizes = [math.prod(item.shape) for item in small]
    packed = jnp.concatenate([item.reshape(-1) for item in small])
    gathered = lax.all_gather(packed, "fsdp", axis=0)
    full = []
    offset = 0
    for size in sizes:
        full.append(gathered[:, offset : offset + size].astype(f32))
        offset += size
    gain_one, shift_one, bias_pair, bias_proj, scale_one = full[:5]
    gain_two, shift_two, bias_up, bias_down, scale_two = full[5:]
    gain_one, shift_one, bias_proj, scale_one, gain_two, shift_two, bias_down, scale_two = [
        item.reshape(1, features)
        for item in (
            gain_one, shift_one, bias_proj, scale_one, gain_two, shift_two, bias_down, scale_two
        )
    ]
    bias_pair = (
        bias_pair.reshape(shards, 2, heads, -1).transpose(1, 2, 0, 3).reshape(2, width)
    )
    bias_up = bias_up.reshape(shards, up_bias.shape[0], -1).transpose(1, 0, 2).reshape(1, inner)

    attn_part = jnp.concatenate(
        [qkv_weight.reshape(qkv_weight.shape[0], 3 * width), proj_weight.T], axis=1
    )
    attn_full = lax.all_gather(attn_part, "fsdp", axis=0, tiled=True)
    qkv_matrix = attn_full[:, : 3 * width]
    proj_back = attn_full[:, 3 * width :]
    piece = up_weight.shape[0] // groups
    up_piece = lax.dynamic_slice_in_dim(up_weight, place * piece, piece, 0)
    down_piece = lax.dynamic_slice_in_dim(down_weight, place * piece, piece, 1)
    mlp_full = lax.all_gather(
        jnp.concatenate([up_piece, down_piece.T], axis=1), ("fsdp", "ctx"), axis=0, tiled=True
    )
    up_full = mlp_full[:, :inner]
    down_back = mlp_full[:, inner:]

    source = inputs.reshape(slots, features).astype(f32)
    normed_one, unit_one, inverse_one = normalize(source, gain_one, shift_one)
    low_one = normed_one.astype(bf16)
    bias_kv = jnp.concatenate([jnp.zeros((width,), f32), bias_pair[1]])
    own = (dot(low_one, qkv_matrix[:, width:], ((1,), (0,))) + bias_kv).astype(bf16)
    others = [ring_shift(own, "ctx", step) for step in range(1, groups)]
    queries = (dot(low_one, qkv_matrix[:, :width], ((1,), (0,))) + bias_pair[0]).astype(bf16)
    order = (place - jnp.arange(groups, dtype=jnp.int32)) % groups
    live = jnp.take(lengths[0], order)
    mixed = attend(live, queries, own, others, head_size)

    proj_part = dot(mixed, proj_back, ((1,), (1,))).astype(bf16)
    projected = exchange_sum(proj_part, "tp") + bias_proj
    resid = source + scale_one * projected
    normed_two, unit_two, inverse_two = normalize(resid, gain_two, shift_two)
    low_two = normed_two.astype(bf16)
    hidden = dot(low_two, up_full, ((1,), (0,))) + bias_up
    cumulative, derivative = gelu_parts(hidden)
    activated = (hidden * cumulative).astype(bf16)

    row = lax.broadcasted_iota(jnp.int32, (slots, 1), 0)
    live_rows = (row < live[0]).astype(f32)
    upstream = cotangent.reshape(slots, features) * live_rows
    dmlp = upstream * scale_two
    grad_down_bias = jnp.sum(dmlp, axis=0)
    dmlp_low = dmlp.astype(bf16)
    dhidden = dot(dmlp_low, down_back, ((1,), (0,))) * derivative
    grad_up_bias = jnp.sum(dhidden, axis=0)
    dhidden_low = dhidden.astype(bf16)
    dnorm_part = dot(dhidden_low, up_full, ((1,), (1,))).astype(bf16)
    dnorm_other = swap_pair(dnorm_part, "tp")
    up_part = dot(low_two, dhidden_low, ((0,), (0,))).astype(bf16)
    down_grad_part = dot(dmlp_low, activated, ((0,), (0,))).astype(bf16)
    down_part = dot(activated, down_back, ((1,), (1,))).astype(bf16)
    dnorm_other = after(dnorm_other, up_part, down_grad_part, down_part)
    dnorm_two = pair_sum(dnorm_part, dnorm_other, "tp")
    mlp_other = swap_pair(down_part, "tp")

    def reduce_shards(matrix):
        return lax.psum_scatter(matrix, "fsdp", scatter_dimension=0, tiled=True)

    down_shard = reduce_shards(down_grad_part)

    grad_gain_two = jnp.sum(dnorm_two * unit_two, axis=0)
    grad_shift_two = jnp.sum(dnorm_two, axis=0)
    dresid = upstream + normalize_back(dnorm_two, unit_two, inverse_two, gain_two)
    grad_scale_one = jnp.sum(dresid * projected, axis=0)
    dproj = dresid * scale_one
    grad_proj_bias = jnp.sum(dproj, axis=0)
    dproj_low = dproj.astype(bf16)
    dmixed = dot(dproj_low, proj_back, ((1,), (0,))).astype(bf16)
    proj_grad_part = dot(dproj_low, mixed, ((0,), (0,))).astype(bf16)
    up_shard = reduce_shards(jnp.concatenate([up_part, proj_grad_part], axis=1))

    query_grad, own_grad, *sent = attend_back(live, queries, dmixed, own, others, head_size)
    mlp_other = after(mlp_other, query_grad)
    mlp_out = pair_sum(down_part, mlp_other, "tp") + bias_down
    output = (resid + scale_two * mlp_out).astype(bf16).reshape(images, slots, features)
    grad_scale_two = jnp.sum(upstream * mlp_out, axis=0)
    for step, item in enumerate(sent):
        own_grad = own_grad + ring_shift(item, "ctx", -(step + 1)).astype(f32)
    own_low = own_grad.astype(bf16)
    dqkv = jnp.concatenate([query_grad, own_low[0], own_low[1]], axis=1)
    dnorm_local = dot(dqkv, qkv_matrix, ((1,), (1,))).astype(bf16)
    dnorm_one = exchange_sum(dnorm_local, "tp")
    qkv_part = dot(low_one, dqkv, ((0,), (0,))).astype(bf16)
    qkv_shard = reduce_shards(qkv_part)
    grad_down = exchange_sum(down_shard, "ctx").T
    up_sum = exchange_sum(up_shard, "ctx")
    grad_up = up_sum[:, :inner]
    grad_proj = up_sum[:, inner:].T
    grad_qkv = exchange_sum(after(qkv_shard, up_sum, grad_down), "ctx")
    grad_qkv_bias = jnp.stack(
        [jnp.sum(query_grad.astype(f32), axis=0), jnp.sum(own_low[1].astype(f32), axis=0)]
    )
    grad_gain_one = jnp.sum(dnorm_one * unit_one, axis=0)
    grad_shift_one = jnp.sum(dnorm_one, axis=0)
    dinput = (
        (dresid + normalize_back(dnorm_one, unit_one, inverse_one, gain_one))
        .astype(bf16)
        .reshape(images, slots, features)
    )

    pieces = [
        grad_gain_one,
        grad_shift_one,
        grad_qkv_bias.reshape(2, heads, shards, -1).transpose(2, 0, 1, 3),
        grad_proj_bias,
        grad_scale_one,
        grad_gain_two,
        grad_shift_two,
        grad_up_bias.reshape(up_bias.shape[0], shards, -1).transpose(1, 0, 2),
        grad_down_bias,
        grad_scale_two,
    ]
    sent_small = jnp.concatenate([item.reshape(shards, -1) for item in pieces], axis=1)
    got = lax.all_to_all(sent_small.astype(bf16), "fsdp", split_axis=0, concat_axis=0, tiled=True)
    total = exchange_sum(jnp.sum(got.astype(f32), axis=0).astype(bf16), "ctx")
    results = []
    offset = 0
    for item, size in zip(small, sizes):
        results.append(total[offset : offset + size].reshape(item.shape))
        offset += size
    (
        out_gain_one,
        out_shift_one,
        out_qkv_bias,
        out_proj_bias,
        out_scale_one,
        out_gain_two,
        out_shift_two,
        out_up_bias,
        out_down_bias,
        out_scale_two,
    ) = results
    return (
        output,
        dinput,
        out_gain_one,
        out_shift_one,
        grad_qkv.reshape(qkv_weight.shape),
        out_qkv_bias,
        grad_proj,
        out_proj_bias,
        out_scale_one,
        out_gain_two,
        out_shift_two,
        grad_up,
        out_up_bias,
        grad_down,
        out_down_bias,
        out_scale_two,
    )


def solution(mesh):
    rows = P("fsdp", "ctx", None)
    vector = P("fsdp")
    params = (
        vector,
        vector,
        P("fsdp", None, "tp"),
        P(None, "tp", "fsdp"),
        P("tp", "fsdp"),
        vector,
        vector,
        vector,
        vector,
        P("fsdp", "tp"),
        P("tp", "fsdp"),
        P("tp", "fsdp"),
        vector,
        vector,
    )

    return jax.shard_map(
        body,
        mesh=mesh,
        in_specs=(rows, P("fsdp", None)) + params + (rows,),
        out_specs=(rows, rows) + params,
        check_vma=False,
    )
```

```python
import math

import jax
import jax.numpy as jnp
from jax import lax
from jax.experimental import pallas as pl
from jax.experimental.pallas import tpu as pltpu
from jax.sharding import PartitionSpec as P

epsilon = 1e-06
negative = -1e30
f32 = jnp.float32
bf16 = jnp.bfloat16


def normalize(values, gain, shift):
    center = values - jnp.mean(values, axis=-1, keepdims=True)
    inverse = lax.rsqrt(jnp.mean(center * center, axis=-1, keepdims=True) + epsilon)
    standard = center * inverse
    return (standard * gain + shift, standard, inverse)


def normalize_back(upstream, standard, inverse, gain):
    scaled = upstream * gain
    return inverse * (
        scaled
        - jnp.mean(scaled, axis=-1, keepdims=True)
        - standard * jnp.mean(scaled * standard, axis=-1, keepdims=True)
    )


def gelu_parts(hidden):
    cumulative = 0.5 * (1.0 + jax.scipy.special.erf(hidden * (1.0 / math.sqrt(2.0))))
    density = jnp.exp(-0.5 * hidden * hidden) * (1.0 / math.sqrt(2.0 * math.pi))
    return (cumulative, cumulative + hidden * density)


def dot(left, right, dims):
    return lax.dot_general(left, right, (dims, ((), ())), preferred_element_type=f32)


def swap_pair(part, axis):
    if lax.axis_size(axis) == 2:
        return lax.ppermute(part, axis, [(0, 1), (1, 0)])
    return None


def pair_sum(part, other, axis):
    if other is None:
        return lax.psum(part, axis).astype(f32)
    return part.astype(f32) + other.astype(f32)


def exchange_sum(part, axis):
    return pair_sum(part, swap_pair(part, axis), axis)


def after(value, *events):
    if value is None:
        return None
    return lax.optimization_barrier((value,) + events)[0]


def ring_shift(value, axis, step):
    size = lax.axis_size(axis)
    return lax.ppermute(value, axis, [(i, (i + step) % size) for i in range(size)])


def head_mask(rows, width, head_size, head):
    lane = lax.broadcasted_iota(jnp.int32, (rows, width), 1)
    return (lane // head_size == head).astype(f32)


def forward_kernel(live_ref, query_ref, *rest, head_size, blocks):
    key_refs, value_refs, out_ref = rest[:blocks], rest[blocks : 2 * blocks], rest[-1]
    rows, width = query_ref.shape
    column = lax.broadcasted_iota(jnp.int32, (1, blocks * rows), 1)
    usable = column < 0
    for i in range(blocks):
        usable = usable | ((column >= i * rows) & (column < i * rows + live_ref[i]))
    out_ref[...] = jnp.zeros((rows, width), bf16)

    def one_head(head, carry):
        mask = head_mask(rows, width, head_size, head)
        query = query_ref[...].astype(f32) * (mask * head_size ** (-0.5))
        keys = jnp.concatenate([ref[...] for ref in key_refs], axis=0)
        values = jnp.concatenate([ref[...] for ref in value_refs], axis=0)
        scores = dot(query.astype(bf16), keys, ((1,), (1,)))
        scores = jnp.where(usable, scores, negative)
        maximum = jnp.max(scores, axis=-1, keepdims=True)
        exponent = jnp.exp(scores - maximum)
        summed = jnp.sum(exponent, axis=-1, keepdims=True)
        weights = (exponent * (1.0 / summed)).astype(bf16)
        result = dot(weights, values, ((1,), (0,))) * mask
        out_ref[...] = (out_ref[...].astype(f32) + result).astype(bf16)
        return carry

    lax.fori_loop(0, width // head_size, one_head, 0)


def backward_kernel(live_ref, query_ref, grad_ref, *rest, head_size, blocks):
    key_refs, value_refs = rest[:blocks], rest[blocks : 2 * blocks]
    query_grad_ref = rest[2 * blocks]
    grad_refs = rest[2 * blocks + 1 :]
    rows, width = query_ref.shape
    scaling = head_size ** (-0.5)
    key_position = lax.broadcasted_iota(jnp.int32, (rows, 1), 0)
    query_grad_ref[...] = jnp.zeros((rows, width), query_grad_ref.dtype)
    for ref in grad_refs:
        ref[...] = jnp.zeros((2, rows, width), ref.dtype)

    def one_head(head, carry):
        mask = head_mask(rows, width, head_size, head)
        query = query_ref[...].astype(f32)
        head_query = (query * mask).astype(bf16)
        scaled_query = (query * (mask * scaling)).astype(bf16)
        head_grads = (grad_ref[...].astype(f32) * mask).astype(bf16)
        scores = [
            jnp.where(
                key_position < live_ref[i],
                dot(key_refs[i][...], scaled_query, ((1,), (1,))),
                negative,
            )
            for i in range(blocks)
        ]
        maximum = scores[0].max(axis=0, keepdims=True)
        for item in scores[1:]:
            maximum = jnp.maximum(maximum, item.max(axis=0, keepdims=True))
        exponents = [jnp.exp(item - maximum) for item in scores]
        summed = sum(item.sum(axis=0, keepdims=True) for item in exponents)
        share = 1.0 / summed
        probabilities = [item * share for item in exponents]
        dprobs = [dot(value_refs[i][...], head_grads, ((1,), (1,))) for i in range(blocks)]
        row_total = sum(
            (p * d).sum(axis=0, keepdims=True) for p, d in zip(probabilities, dprobs)
        )
        query_grad = query_grad_ref[...].astype(f32)
        for i, ref in enumerate(grad_refs):
            value_grad = dot(probabilities[i].astype(bf16), head_grads, ((1,), (0,)))
            ref[1] = (ref[1].astype(f32) + value_grad).astype(ref.dtype)
            dscores = (probabilities[i] * (dprobs[i] - row_total) * scaling).astype(bf16)
            key_grad = dot(dscores, head_query, ((1,), (0,)))
            ref[0] = (ref[0].astype(f32) + key_grad).astype(ref.dtype)
            query_grad = query_grad + dot(dscores, key_refs[i][...], ((0,), (0,))) * mask
        query_grad_ref[...] = query_grad.astype(bf16)
        return carry

    lax.fori_loop(0, width // head_size, one_head, 0)


def column_block(rows, width, first):
    return pl.BlockSpec((rows, width), lambda p: (0, first + p))


def attend(live, query, own, others, head_size, interpret=False):
    rows, local = query.shape
    width = 2 * head_size
    pairs = local // width
    sources = [own] + list(others)
    blocks = len(sources)
    return pl.pallas_call(
        lambda *refs: forward_kernel(*refs, head_size=head_size, blocks=blocks),
        grid=(pairs,),
        in_specs=[pl.BlockSpec(memory_space=pltpu.SMEM), column_block(rows, width, 0)]
        + [column_block(rows, width, 0)] * blocks
        + [column_block(rows, width, pairs)] * blocks,
        out_specs=column_block(rows, width, 0),
        out_shape=jax.ShapeDtypeStruct((rows, local), bf16),
        cost_estimate=pl.CostEstimate(
            flops=4 * rows * rows * blocks * local,
            bytes_accessed=2 * rows * local * (2 + 2 * blocks),
            transcendentals=rows * rows * blocks * local // head_size,
        ),
        compiler_params=pltpu.CompilerParams(vmem_limit_bytes=56 * 1024 * 1024),
        name="attend",
        interpret=interpret,
    )(live, query, *sources, *sources)


def attend_back(live, query, grads, own, others, head_size, interpret=False):
    rows, local = query.shape
    width = 2 * head_size
    pairs = local // width
    sources = [own] + list(others)
    blocks = len(sources)
    stacked = pl.BlockSpec((2, rows, width), lambda p: (0, 0, p))
    return pl.pallas_call(
        lambda *refs: backward_kernel(*refs, head_size=head_size, blocks=blocks),
        grid=(pairs,),
        in_specs=[pl.BlockSpec(memory_space=pltpu.SMEM)]
        + [column_block(rows, width, 0)] * 2
        + [column_block(rows, width, 0)] * blocks
        + [column_block(rows, width, pairs)] * blocks,
        out_specs=[column_block(rows, width, 0)] + [stacked] * blocks,
        out_shape=[
            jax.ShapeDtypeStruct((rows, local), bf16),
            jax.ShapeDtypeStruct((2, rows, local), f32),
        ]
        + [jax.ShapeDtypeStruct((2, rows, local), bf16)] * (blocks - 1),
        cost_estimate=pl.CostEstimate(
            flops=10 * rows * rows * blocks * local,
            bytes_accessed=2 * rows * local * (3 + 6 * blocks),
            transcendentals=rows * rows * blocks * local // head_size,
        ),
        compiler_params=pltpu.CompilerParams(vmem_limit_bytes=56 * 1024 * 1024),
        name="attend_back",
        interpret=interpret,
    )(live, query, grads, *sources, *sources)


def body(
    inputs,
    lengths,
    first_gain,
    first_shift,
    qkv_weight,
    qkv_bias,
    proj_weight,
    proj_bias,
    attn_scale,
    second_gain,
    second_shift,
    up_weight,
    up_bias,
    down_weight,
    down_bias,
    mlp_scale,
    cotangent,
):
    images, slots, features = inputs.shape
    assert images == 1
    shards = lax.axis_size("fsdp")
    groups = lax.axis_size("ctx")
    place = lax.axis_index("ctx")
    width = qkv_weight.shape[2]
    inner = up_weight.shape[1]
    heads = qkv_bias.shape[1]
    head_size = qkv_bias.shape[2] * shards

    small = [
        first_gain,
        first_shift,
        qkv_bias,
        proj_bias,
        attn_scale,
        second_gain,
        second_shift,
        up_bias,
        down_bias,
        mlp_scale,
    ]
    sizes = [math.prod(item.shape) for item in small]
    packed = jnp.concatenate([item.reshape(-1) for item in small])
    gathered = lax.all_gather(packed, "fsdp", axis=0)
    full = []
    offset = 0
    for size in sizes:
        full.append(gathered[:, offset : offset + size].astype(f32))
        offset += size
    gain_one, shift_one, bias_pair, bias_proj, scale_one = full[:5]
    gain_two, shift_two, bias_up, bias_down, scale_two = full[5:]
    gain_one, shift_one, bias_proj, scale_one, gain_two, shift_two, bias_down, scale_two = [
        item.reshape(1, features)
        for item in (
            gain_one, shift_one, bias_proj, scale_one, gain_two, shift_two, bias_down, scale_two
        )
    ]
    bias_pair = (
        bias_pair.reshape(shards, 2, heads, -1).transpose(1, 2, 0, 3).reshape(2, width)
    )
    bias_up = bias_up.reshape(shards, up_bias.shape[0], -1).transpose(1, 0, 2).reshape(1, inner)

    attn_part = jnp.concatenate(
        [qkv_weight.reshape(qkv_weight.shape[0], 3 * width), proj_weight.T], axis=1
    )
    attn_full = lax.all_gather(attn_part, "fsdp", axis=0, tiled=True)
    qkv_matrix = attn_full[:, : 3 * width]
    proj_back = attn_full[:, 3 * width :]
    piece = up_weight.shape[0] // groups
    up_piece = lax.dynamic_slice_in_dim(up_weight, place * piece, piece, 0)
    down_piece = lax.dynamic_slice_in_dim(down_weight, place * piece, piece, 1)
    mlp_full = lax.all_gather(
        jnp.concatenate([up_piece, down_piece.T], axis=1), ("fsdp", "ctx"), axis=0, tiled=True
    )
    up_full = mlp_full[:, :inner]
    down_back = mlp_full[:, inner:]

    source = inputs.reshape(slots, features).astype(f32)
    normed_one, unit_one, inverse_one = normalize(source, gain_one, shift_one)
    low_one = normed_one.astype(bf16)
    bias_kv = jnp.concatenate([jnp.zeros((width,), f32), bias_pair[1]])
    own = (dot(low_one, qkv_matrix[:, width:], ((1,), (0,))) + bias_kv).astype(bf16)
    others = [ring_shift(own, "ctx", step) for step in range(1, groups)]
    queries = (dot(low_one, qkv_matrix[:, :width], ((1,), (0,))) + bias_pair[0]).astype(bf16)
    order = (place - jnp.arange(groups, dtype=jnp.int32)) % groups
    live = jnp.take(lengths[0], order)
    mixed = attend(live, queries, own, others, head_size)

    proj_part = dot(mixed, proj_back, ((1,), (1,))).astype(bf16)
    projected = exchange_sum(proj_part, "tp") + bias_proj
    resid = source + scale_one * projected
    normed_two, unit_two, inverse_two = normalize(resid, gain_two, shift_two)
    low_two = normed_two.astype(bf16)
    hidden = dot(low_two, up_full, ((1,), (0,))) + bias_up
    cumulative, derivative = gelu_parts(hidden)
    activated = (hidden * cumulative).astype(bf16)

    row = lax.broadcasted_iota(jnp.int32, (slots, 1), 0)
    live_rows = (row < live[0]).astype(f32)
    upstream = cotangent.reshape(slots, features) * live_rows
    dmlp = upstream * scale_two
    grad_down_bias = jnp.sum(dmlp, axis=0)
    dmlp_low = dmlp.astype(bf16)
    dhidden = dot(dmlp_low, down_back, ((1,), (0,))) * derivative
    grad_up_bias = jnp.sum(dhidden, axis=0)
    dhidden_low = dhidden.astype(bf16)
    dnorm_part = dot(dhidden_low, up_full, ((1,), (1,))).astype(bf16)
    dnorm_other = swap_pair(dnorm_part, "tp")
    up_part = dot(low_two, dhidden_low, ((0,), (0,))).astype(bf16)
    down_grad_part = dot(dmlp_low, activated, ((0,), (0,))).astype(bf16)
    down_part = dot(activated, down_back, ((1,), (1,))).astype(bf16)
    dnorm_other = after(dnorm_other, up_part, down_grad_part, down_part)
    dnorm_two = pair_sum(dnorm_part, dnorm_other, "tp")
    mlp_other = swap_pair(down_part, "tp")

    def reduce_shards(matrix):
        return lax.psum_scatter(matrix, "fsdp", scatter_dimension=0, tiled=True)

    down_shard = reduce_shards(down_grad_part)

    grad_gain_two = jnp.sum(dnorm_two * unit_two, axis=0)
    grad_shift_two = jnp.sum(dnorm_two, axis=0)
    dresid = upstream + normalize_back(dnorm_two, unit_two, inverse_two, gain_two)
    grad_scale_one = jnp.sum(dresid * projected, axis=0)
    dproj = dresid * scale_one
    grad_proj_bias = jnp.sum(dproj, axis=0)
    dproj_low = dproj.astype(bf16)
    dmixed = dot(dproj_low, proj_back, ((1,), (0,))).astype(bf16)
    proj_grad_part = dot(dproj_low, mixed, ((0,), (0,))).astype(bf16)
    up_shard = reduce_shards(jnp.concatenate([up_part, proj_grad_part], axis=1))

    query_grad, own_grad, *sent = attend_back(live, queries, dmixed, own, others, head_size)
    mlp_other = after(mlp_other, query_grad)
    mlp_out = pair_sum(down_part, mlp_other, "tp") + bias_down
    output = (resid + scale_two * mlp_out).astype(bf16).reshape(images, slots, features)
    grad_scale_two = jnp.sum(upstream * mlp_out, axis=0)
    for step, item in enumerate(sent):
        own_grad = own_grad + ring_shift(item, "ctx", -(step + 1)).astype(f32)
    own_low = own_grad.astype(bf16)
    dqkv = jnp.concatenate([query_grad, own_low[0], own_low[1]], axis=1)
    dnorm_local = dot(dqkv, qkv_matrix, ((1,), (1,)))
    grad_gain_one = jnp.sum(dnorm_local * unit_one, axis=0)
    grad_shift_one = jnp.sum(dnorm_local, axis=0)
    dnorm_low = dnorm_local.astype(bf16)
    dnorm_other = swap_pair(dnorm_low, "tp")
    dnorm_one = pair_sum(dnorm_low, dnorm_other, "tp")
    qkv_part = dot(low_one, dqkv, ((0,), (0,))).astype(bf16)
    qkv_shard = reduce_shards(qkv_part)
    down_other = swap_pair(down_shard, "ctx")
    up_other = swap_pair(up_shard, "ctx")
    grad_down = pair_sum(down_shard, down_other, "ctx").T
    up_sum = pair_sum(up_shard, up_other, "ctx")
    grad_up = up_sum[:, :inner]
    grad_proj = up_sum[:, inner:].T
    grad_qkv = exchange_sum(after(qkv_shard, up_sum, grad_down), "ctx")
    grad_qkv_bias = jnp.stack(
        [jnp.sum(query_grad.astype(f32), axis=0), jnp.sum(own_low[1].astype(f32), axis=0)]
    )
    dinput = (
        (dresid + normalize_back(dnorm_one, unit_one, inverse_one, gain_one))
        .astype(bf16)
        .reshape(images, slots, features)
    )

    pieces = [
        grad_gain_one,
        grad_shift_one,
        grad_qkv_bias.reshape(2, heads, shards, -1).transpose(2, 0, 1, 3),
        grad_proj_bias,
        grad_scale_one,
        grad_gain_two,
        grad_shift_two,
        grad_up_bias.reshape(up_bias.shape[0], shards, -1).transpose(1, 0, 2),
        grad_down_bias,
        grad_scale_two,
    ]
    sent_small = jnp.concatenate([item.reshape(shards, -1) for item in pieces], axis=1)
    got = lax.all_to_all(sent_small.astype(bf16), "fsdp", split_axis=0, concat_axis=0, tiled=True)
    total = jnp.sum(got.astype(f32), axis=0).astype(bf16)
    total = exchange_sum(total, "ctx")
    halves = sizes[0] + sizes[1]
    first_part = exchange_sum(total[:halves].astype(bf16), "tp")
    total = jnp.concatenate([first_part, total[halves:]])
    results = []
    offset = 0
    for item, size in zip(small, sizes):
        results.append(total[offset : offset + size].reshape(item.shape))
        offset += size
    (
        out_gain_one,
        out_shift_one,
        out_qkv_bias,
        out_proj_bias,
        out_scale_one,
        out_gain_two,
        out_shift_two,
        out_up_bias,
        out_down_bias,
        out_scale_two,
    ) = results
    return (
        output,
        dinput,
        out_gain_one,
        out_shift_one,
        grad_qkv.reshape(qkv_weight.shape),
        out_qkv_bias,
        grad_proj,
        out_proj_bias,
        out_scale_one,
        out_gain_two,
        out_shift_two,
        grad_up,
        out_up_bias,
        grad_down,
        out_down_bias,
        out_scale_two,
    )


def solution(mesh):
    rows = P("fsdp", "ctx", None)
    vector = P("fsdp")
    params = (
        vector,
        vector,
        P("fsdp", None, "tp"),
        P(None, "tp", "fsdp"),
        P("tp", "fsdp"),
        vector,
        vector,
        vector,
        vector,
        P("fsdp", "tp"),
        P("tp", "fsdp"),
        P("tp", "fsdp"),
        vector,
        vector,
    )

    return jax.shard_map(
        body,
        mesh=mesh,
        in_specs=(rows, P("fsdp", None)) + params + (rows,),
        out_specs=(rows, rows) + params,
        check_vma=False,
    )
```

```python
import math

import jax
import jax.numpy as jnp
from jax import lax
from jax.experimental import pallas as pl
from jax.experimental.pallas import tpu as pltpu
from jax.experimental.layout import Layout, with_layout_constraint
from jax.sharding import PartitionSpec as P


epsilon = 1e-06
negative = -1e30
f32 = jnp.float32
bf16 = jnp.bfloat16


def normalize(values, gain, shift):
    center = values - jnp.mean(values, axis=-1, keepdims=True)
    inverse = lax.rsqrt(jnp.mean(center * center, axis=-1, keepdims=True) + epsilon)
    standard = center * inverse
    return (standard * gain + shift, standard, inverse)


def normalize_back(upstream, standard, inverse, gain):
    scaled = upstream * gain
    return inverse * (
        scaled
        - jnp.mean(scaled, axis=-1, keepdims=True)
        - standard * jnp.mean(scaled * standard, axis=-1, keepdims=True)
    )


def gelu_parts(hidden):
    cumulative = 0.5 * (1.0 + jax.scipy.special.erf(hidden * (1.0 / math.sqrt(2.0))))
    density = jnp.exp(-0.5 * hidden * hidden) * (1.0 / math.sqrt(2.0 * math.pi))
    return (cumulative, cumulative + hidden * density)


def dot(left, right, dims):
    return lax.dot_general(left, right, (dims, ((), ())), preferred_element_type=f32)


def swap_pair(part, axis):
    if lax.axis_size(axis) == 2:
        return lax.ppermute(part, axis, [(0, 1), (1, 0)])
    return None


def pair_sum(part, other, axis):
    if other is None:
        return lax.psum(part, axis).astype(f32)
    return part.astype(f32) + other.astype(f32)


def exchange_sum(part, axis):
    return pair_sum(part, swap_pair(part, axis), axis)


def rows_major(matrix):
    return with_layout_constraint(matrix, Layout(major_to_minor=(0, 1)))


def after(value, *events):
    if value is None:
        return None
    return lax.optimization_barrier((value,) + events)[0]


def ring_shift(value, axis, step):
    size = lax.axis_size(axis)
    return lax.ppermute(value, axis, [(i, (i + step) % size) for i in range(size)])


def head_mask(rows, width, head_size, head):
    lane = lax.broadcasted_iota(jnp.int32, (rows, width), 1)
    return (lane // head_size == head).astype(f32)


def forward_kernel(live_ref, query_ref, *rest, head_size, blocks):
    key_refs, value_refs, out_ref = rest[:blocks], rest[blocks : 2 * blocks], rest[-1]
    rows, width = query_ref.shape
    column = lax.broadcasted_iota(jnp.int32, (1, blocks * rows), 1)
    usable = column < 0
    for i in range(blocks):
        usable = usable | ((column >= i * rows) & (column < i * rows + live_ref[i]))
    bias = jnp.where(usable, 0.0, negative)
    query = query_ref[...].astype(f32)
    keys = jnp.concatenate([ref[...] for ref in key_refs], axis=0)
    values = jnp.concatenate([ref[...] for ref in value_refs], axis=0)
    result = jnp.zeros((rows, width), f32)
    for head in range(width // head_size):
        mask = head_mask(rows, width, head_size, head)
        scores = dot((query * (mask * head_size ** (-0.5))).astype(bf16), keys, ((1,), (1,)))
        scores = scores + bias
        maximum = jnp.max(scores, axis=-1, keepdims=True)
        exponent = jnp.exp(scores - maximum)
        summed = jnp.sum(exponent, axis=-1, keepdims=True)
        attended = dot(exponent.astype(bf16), values, ((1,), (0,)))
        result = result + attended * (mask * (1.0 / summed))
    out_ref[...] = result.astype(bf16)


def backward_kernel(live_ref, query_ref, grad_ref, *rest, head_size, blocks):
    key_refs, value_refs = rest[:blocks], rest[blocks : 2 * blocks]
    query_grad_ref = rest[2 * blocks]
    grad_refs = rest[2 * blocks + 1 :]
    rows, width = query_ref.shape
    scaling = head_size ** (-0.5)
    key_position = lax.broadcasted_iota(jnp.int32, (rows, 1), 0)
    query_grad_ref[...] = jnp.zeros((rows, width), query_grad_ref.dtype)
    for ref in grad_refs:
        ref[...] = jnp.zeros((2, rows, width), ref.dtype)

    def one_head(head, carry):
        mask = head_mask(rows, width, head_size, head)
        query = query_ref[...].astype(f32)
        head_query = (query * mask).astype(bf16)
        scaled_query = (query * (mask * scaling)).astype(bf16)
        head_grads = (grad_ref[...].astype(f32) * mask).astype(bf16)
        scores = [
            jnp.where(
                key_position < live_ref[i],
                dot(key_refs[i][...], scaled_query, ((1,), (1,))),
                negative,
            )
            for i in range(blocks)
        ]
        maximum = scores[0].max(axis=0, keepdims=True)
        for item in scores[1:]:
            maximum = jnp.maximum(maximum, item.max(axis=0, keepdims=True))
        exponents = [jnp.exp(item - maximum) for item in scores]
        summed = sum(item.sum(axis=0, keepdims=True) for item in exponents)
        share = 1.0 / summed
        probabilities = [item * share for item in exponents]
        dprobs = [dot(value_refs[i][...], head_grads, ((1,), (1,))) for i in range(blocks)]
        row_total = sum(
            (p * d).sum(axis=0, keepdims=True) for p, d in zip(probabilities, dprobs)
        )
        query_grad = query_grad_ref[...].astype(f32)
        for i, ref in enumerate(grad_refs):
            value_grad = dot(probabilities[i].astype(bf16), head_grads, ((1,), (0,)))
            ref[1] = (ref[1].astype(f32) + value_grad).astype(ref.dtype)
            dscores = (probabilities[i] * (dprobs[i] - row_total) * scaling).astype(bf16)
            key_grad = dot(dscores, head_query, ((1,), (0,)))
            ref[0] = (ref[0].astype(f32) + key_grad).astype(ref.dtype)
            query_grad = query_grad + dot(dscores, key_refs[i][...], ((0,), (0,))) * mask
        query_grad_ref[...] = query_grad.astype(bf16)
        return carry

    lax.fori_loop(0, width // head_size, one_head, 0)


def column_block(rows, width, first):
    return pl.BlockSpec((rows, width), lambda p: (0, first + p))


def attend(live, query, own, others, head_size, interpret=False):
    rows, local = query.shape
    width = 2 * head_size
    pairs = local // width
    sources = [own] + list(others)
    blocks = len(sources)
    return pl.pallas_call(
        lambda *refs: forward_kernel(*refs, head_size=head_size, blocks=blocks),
        grid=(pairs,),
        in_specs=[pl.BlockSpec(memory_space=pltpu.SMEM), column_block(rows, width, 0)]
        + [column_block(rows, width, 0)] * blocks
        + [column_block(rows, width, pairs)] * blocks,
        out_specs=column_block(rows, width, 0),
        out_shape=jax.ShapeDtypeStruct((rows, local), bf16),
        cost_estimate=pl.CostEstimate(
            flops=4 * rows * rows * blocks * local,
            bytes_accessed=2 * rows * local * (2 + 2 * blocks),
            transcendentals=rows * rows * blocks * local // head_size,
        ),
        compiler_params=pltpu.CompilerParams(vmem_limit_bytes=56 * 1024 * 1024),
        name="attend",
        interpret=interpret,
    )(live, query, *sources, *sources)


def attend_back(live, query, grads, own, others, head_size, first, count, interpret=False):
    rows, full = query.shape
    width = 2 * head_size
    local = count * width
    pairs = full // width
    sources = [own] + list(others)
    blocks = len(sources)
    stacked = pl.BlockSpec((2, rows, width), lambda p: (0, 0, p))
    return pl.pallas_call(
        lambda *refs: backward_kernel(*refs, head_size=head_size, blocks=blocks),
        grid=(count,),
        in_specs=[pl.BlockSpec(memory_space=pltpu.SMEM)]
        + [column_block(rows, width, first)] * 2
        + [column_block(rows, width, first)] * blocks
        + [column_block(rows, width, pairs + first)] * blocks,
        out_specs=[column_block(rows, width, 0)] + [stacked] * blocks,
        out_shape=[
            jax.ShapeDtypeStruct((rows, local), bf16),
            jax.ShapeDtypeStruct((2, rows, local), f32),
        ]
        + [jax.ShapeDtypeStruct((2, rows, local), bf16)] * (blocks - 1),
        cost_estimate=pl.CostEstimate(
            flops=10 * rows * rows * blocks * local,
            bytes_accessed=2 * rows * local * (3 + 6 * blocks),
            transcendentals=rows * rows * blocks * local // head_size,
        ),
        compiler_params=pltpu.CompilerParams(vmem_limit_bytes=56 * 1024 * 1024),
        interpret=interpret,
    )(live, query, grads, *sources, *sources)


def body(
    inputs,
    lengths,
    first_gain,
    first_shift,
    qkv_weight,
    qkv_bias,
    proj_weight,
    proj_bias,
    attn_scale,
    second_gain,
    second_shift,
    up_weight,
    up_bias,
    down_weight,
    down_bias,
    mlp_scale,
    cotangent,
):
    images, slots, features = inputs.shape
    assert images == 1
    shards = lax.axis_size("fsdp")
    groups = lax.axis_size("ctx")
    place = lax.axis_index("ctx")
    width = qkv_weight.shape[2]
    inner = up_weight.shape[1]
    heads = qkv_bias.shape[1]
    head_size = qkv_bias.shape[2] * shards

    small = [
        first_gain,
        first_shift,
        qkv_bias,
        proj_bias,
        attn_scale,
        second_gain,
        second_shift,
        up_bias,
        down_bias,
        mlp_scale,
    ]
    sizes = [math.prod(item.shape) for item in small]
    packed = jnp.concatenate([item.reshape(-1) for item in small])
    gathered = lax.all_gather(packed, "fsdp", axis=0)
    full = []
    offset = 0
    for size in sizes:
        full.append(gathered[:, offset : offset + size].astype(f32))
        offset += size
    gain_one, shift_one, bias_pair, bias_proj, scale_one = full[:5]
    gain_two, shift_two, bias_up, bias_down, scale_two = full[5:]
    gain_one, shift_one, bias_proj, scale_one, gain_two, shift_two, bias_down, scale_two = [
        item.reshape(1, features)
        for item in (
            gain_one, shift_one, bias_proj, scale_one, gain_two, shift_two, bias_down, scale_two
        )
    ]
    bias_pair = (
        bias_pair.reshape(shards, 2, heads, -1).transpose(1, 2, 0, 3).reshape(2, width)
    )
    bias_up = bias_up.reshape(shards, up_bias.shape[0], -1).transpose(1, 0, 2).reshape(1, inner)

    attn_part = jnp.concatenate(
        [qkv_weight.reshape(qkv_weight.shape[0], 3 * width), proj_weight.T], axis=1
    )
    attn_full = lax.all_gather(attn_part, "fsdp", axis=0, tiled=True)
    qkv_matrix = attn_full[:, : 3 * width]
    proj_back = attn_full[:, 3 * width :]
    piece = up_weight.shape[0] // groups
    up_piece = lax.dynamic_slice_in_dim(up_weight, place * piece, piece, 0)
    down_piece = lax.dynamic_slice_in_dim(down_weight, place * piece, piece, 1)
    mlp_full = lax.all_gather(
        jnp.concatenate([up_piece, down_piece.T], axis=1), ("fsdp", "ctx"), axis=0, tiled=True
    )
    up_full = mlp_full[:, :inner]
    down_back = mlp_full[:, inner:]

    source = inputs.reshape(slots, features).astype(f32)
    normed_one, unit_one, inverse_one = normalize(source, gain_one, shift_one)
    low_one = normed_one.astype(bf16)
    bias_kv = jnp.concatenate([jnp.zeros((width,), f32), bias_pair[1]])
    own = (dot(low_one, qkv_matrix[:, width:], ((1,), (0,))) + bias_kv).astype(bf16)
    others = [ring_shift(own, "ctx", step) for step in range(1, groups)]
    queries = (dot(low_one, qkv_matrix[:, :width], ((1,), (0,))) + bias_pair[0]).astype(bf16)
    order = (place - jnp.arange(groups, dtype=jnp.int32)) % groups
    live = jnp.take(lengths[0], order)
    mixed = attend(live, queries, own, others, head_size)

    proj_part = dot(mixed, proj_back, ((1,), (1,))).astype(bf16)
    projected = exchange_sum(proj_part, "tp") + bias_proj
    resid = source + scale_one * projected
    normed_two, unit_two, inverse_two = normalize(resid, gain_two, shift_two)
    low_two = normed_two.astype(bf16)
    hidden = dot(low_two, up_full, ((1,), (0,))) + bias_up
    cumulative, derivative = gelu_parts(hidden)
    activated = (hidden * cumulative).astype(bf16)

    row = lax.broadcasted_iota(jnp.int32, (slots, 1), 0)
    live_rows = (row < live[0]).astype(f32)
    upstream = cotangent.reshape(slots, features) * live_rows
    dmlp = upstream * scale_two
    grad_down_bias = jnp.sum(dmlp, axis=0)
    dmlp_low = dmlp.astype(bf16)
    dhidden = dot(dmlp_low, down_back, ((1,), (0,))) * derivative
    grad_up_bias = jnp.sum(dhidden, axis=0)
    dhidden_low = dhidden.astype(bf16)

    def reduce_shards(matrix):
        return lax.psum_scatter(matrix, "fsdp", scatter_dimension=0, tiled=True)

    up_part = dot(low_two, dhidden_low, ((0,), (0,))).astype(bf16)
    up_shard = reduce_shards(up_part)
    dnorm_part = dot(dhidden_low, up_full, ((1,), (1,))).astype(bf16)
    dnorm_other = swap_pair(dnorm_part, "tp")
    part = inner // groups
    if groups == 2:
        sent_units = lax.dynamic_slice_in_dim(activated, (1 - place) * part, part, 1)
        kept_units = lax.dynamic_slice_in_dim(activated, place * part, part, 1)
        down_sent = dot(dmlp_low, sent_units, ((0,), (0,))).astype(bf16)
        down_got = swap_pair(down_sent, "ctx")
        down_kept = dot(dmlp_low, kept_units, ((0,), (0,))).astype(bf16)
        down_half = (down_kept.astype(f32) + down_got.astype(f32)).astype(bf16)
    else:
        down_half = lax.psum_scatter(
            dot(dmlp_low, activated, ((0,), (0,))).astype(bf16),
            "ctx",
            scatter_dimension=1,
            tiled=True,
        )
    down_part = dot(activated, down_back, ((1,), (1,))).astype(bf16)
    dnorm_two = pair_sum(dnorm_part, dnorm_other, "tp")
    mlp_other = swap_pair(down_part, "tp")

    grad_gain_two = jnp.sum(dnorm_two * unit_two, axis=0)
    grad_shift_two = jnp.sum(dnorm_two, axis=0)
    dresid = upstream + normalize_back(dnorm_two, unit_two, inverse_two, gain_two)
    grad_scale_one = jnp.sum(dresid * projected, axis=0)
    dproj = dresid * scale_one
    grad_proj_bias = jnp.sum(dproj, axis=0)
    dproj_low = dproj.astype(bf16)
    dmixed = dot(dproj_low, proj_back, ((1,), (0,))).astype(bf16)
    proj_grad_part = dot(dproj_low, mixed, ((0,), (0,))).astype(bf16)
    down_shard = rows_major(
        reduce_shards(rows_major(jnp.concatenate([down_half, proj_grad_part], axis=1)))
    )

    pairs = width // (2 * head_size)
    cuts = [0, pairs // 2, pairs] if pairs > 1 else [0, pairs]
    query_parts, own_parts = [], []
    for first, last in zip(cuts[:-1], cuts[1:]):
        query_piece, own_grad, *sent = attend_back(
            live, queries, dmixed, own, others, head_size, first, last - first
        )
        query_parts.append(query_piece)
        returned = [
            ring_shift(item, "ctx", -(step + 1)) for step, item in enumerate(sent)
        ]
        own_parts.append((own_grad, returned))
    mlp_other = after(mlp_other, query_parts[-1])
    mlp_out = pair_sum(down_part, mlp_other, "tp") + bias_down
    output = (resid + scale_two * mlp_out).astype(bf16).reshape(images, slots, features)
    grad_scale_two = jnp.sum(upstream * mlp_out, axis=0)
    totals = []
    for own_grad, returned in own_parts:
        for item in returned:
            own_grad = own_grad + item.astype(f32)
        totals.append(own_grad.astype(bf16))
    key_low = [item[0] for item in totals]
    value_low = [item[1] for item in totals]
    dqkv = jnp.concatenate(query_parts + key_low + value_low, axis=1)
    dnorm_local = dot(dqkv, qkv_matrix, ((1,), (1,)))
    grad_gain_one = jnp.sum(dnorm_local * unit_one, axis=0)
    grad_shift_one = jnp.sum(dnorm_local, axis=0)
    dnorm_low = dnorm_local.astype(bf16)
    dnorm_other = swap_pair(dnorm_low, "tp")
    dnorm_one = pair_sum(dnorm_low, dnorm_other, "tp")
    qkv_part = dot(low_one, dqkv, ((0,), (0,))).astype(bf16)
    qkv_shard = reduce_shards(qkv_part)
    up_other = swap_pair(up_shard, "ctx")
    grad_up = pair_sum(up_shard, up_other, "ctx")
    down_other = swap_pair(down_shard, "ctx")
    grad_proj = pair_sum(
        down_shard[:, part:], None if down_other is None else down_other[:, part:], "ctx"
    ).T
    if groups == 2:
        mine, yours = down_shard[:, :part], down_other[:, :part]
        grad_down = jnp.concatenate(
            [jnp.where(place == 0, mine, yours), jnp.where(place == 0, yours, mine)], axis=1
        )
    else:
        grad_down = lax.all_gather(down_shard[:, :part], "ctx", axis=1, tiled=True)
    grad_down = grad_down.astype(f32).T
    grad_qkv = exchange_sum(after(qkv_shard, grad_up, grad_down), "ctx")
    grad_qkv_bias = jnp.concatenate(
        [jnp.sum(item.astype(f32), axis=0) for item in query_parts + value_low]
    )
    dinput = (
        (dresid + normalize_back(dnorm_one, unit_one, inverse_one, gain_one))
        .astype(bf16)
        .reshape(images, slots, features)
    )

    pieces = [
        grad_gain_one,
        grad_shift_one,
        grad_qkv_bias.reshape(2, heads, shards, -1).transpose(2, 0, 1, 3),
        grad_proj_bias,
        grad_scale_one,
        grad_gain_two,
        grad_shift_two,
        grad_up_bias.reshape(up_bias.shape[0], shards, -1).transpose(1, 0, 2),
        grad_down_bias,
        grad_scale_two,
    ]
    sent_small = jnp.concatenate([item.reshape(shards, -1) for item in pieces], axis=1)
    got = lax.all_to_all(sent_small.astype(bf16), "fsdp", split_axis=0, concat_axis=0, tiled=True)
    total = jnp.sum(got.astype(f32), axis=0).astype(bf16)
    total = exchange_sum(total, "ctx")
    halves = sizes[0] + sizes[1]
    first_part = exchange_sum(total[:halves].astype(bf16), "tp")
    total = jnp.concatenate([first_part, total[halves:]])
    results = []
    offset = 0
    for item, size in zip(small, sizes):
        results.append(total[offset : offset + size].reshape(item.shape))
        offset += size
    (
        out_gain_one,
        out_shift_one,
        out_qkv_bias,
        out_proj_bias,
        out_scale_one,
        out_gain_two,
        out_shift_two,
        out_up_bias,
        out_down_bias,
        out_scale_two,
    ) = results
    return (
        output,
        dinput,
        out_gain_one,
        out_shift_one,
        grad_qkv.reshape(qkv_weight.shape),
        out_qkv_bias,
        grad_proj,
        out_proj_bias,
        out_scale_one,
        out_gain_two,
        out_shift_two,
        grad_up,
        out_up_bias,
        grad_down,
        out_down_bias,
        out_scale_two,
    )


def solution(mesh):
    rows = P("fsdp", "ctx", None)
    vector = P("fsdp")
    params = (
        vector,
        vector,
        P("fsdp", None, "tp"),
        P(None, "tp", "fsdp"),
        P("tp", "fsdp"),
        vector,
        vector,
        vector,
        vector,
        P("fsdp", "tp"),
        P("tp", "fsdp"),
        P("tp", "fsdp"),
        vector,
        vector,
    )

    return jax.shard_map(
        body,
        mesh=mesh,
        in_specs=(rows, P("fsdp", None)) + params + (rows,),
        out_specs=(rows, rows) + params,
        check_vma=False,
    )
```

```python
import math

import jax
import jax.numpy as jnp
from jax import lax
from jax.experimental import pallas as pl
from jax.experimental.pallas import tpu as pltpu
from jax.experimental.layout import Layout, with_layout_constraint
from jax.sharding import PartitionSpec as P


epsilon = 1e-06
negative = -1e30
f32 = jnp.float32
bf16 = jnp.bfloat16


def normalize(values, gain, shift):
    center = values - jnp.mean(values, axis=-1, keepdims=True)
    inverse = lax.rsqrt(jnp.mean(center * center, axis=-1, keepdims=True) + epsilon)
    standard = center * inverse
    return (standard * gain + shift, standard, inverse)


def normalize_back(upstream, standard, inverse, gain):
    scaled = upstream * gain
    return inverse * (
        scaled
        - jnp.mean(scaled, axis=-1, keepdims=True)
        - standard * jnp.mean(scaled * standard, axis=-1, keepdims=True)
    )


def gelu_parts(hidden):
    cumulative = 0.5 * (1.0 + jax.scipy.special.erf(hidden * (1.0 / math.sqrt(2.0))))
    density = jnp.exp(-0.5 * hidden * hidden) * (1.0 / math.sqrt(2.0 * math.pi))
    return (cumulative, cumulative + hidden * density)


def dot(left, right, dims):
    return lax.dot_general(left, right, (dims, ((), ())), preferred_element_type=f32)


def swap_pair(part, axis):
    if lax.axis_size(axis) == 2:
        return lax.ppermute(part, axis, [(0, 1), (1, 0)])
    return None


def pair_sum(part, other, axis):
    if other is None:
        return lax.psum(part, axis).astype(f32)
    return part.astype(f32) + other.astype(f32)


def exchange_sum(part, axis):
    return pair_sum(part, swap_pair(part, axis), axis)


def gather_by_permutes(shard, axis):
    size = lax.axis_size(axis)
    index = lax.axis_index(axis)
    steps = size // 2
    rows, columns = shard.shape
    pieces = [shard]
    for k in range(1, steps):
        pieces.append(
            lax.ppermute(shard, axis, [(i, (i + 2 * k) % size) for i in range(size)])
        )
    backward = jnp.concatenate(pieces[::-1] * 2, axis=0)
    start = (steps - 1 - index // 2) * rows
    same = lax.dynamic_slice_in_dim(backward, start, steps * rows, 0)
    other = lax.ppermute(same, axis, [(i, i ^ 1) for i in range(size)])
    same = same.reshape(steps, 1, rows, columns)
    other = other.reshape(steps, 1, rows, columns)
    even = (index % 2 == 0) == (
        lax.broadcasted_iota(jnp.int32, (1, 2, 1, 1), 1) == 0
    )
    full = jnp.where(even, same, other)
    return full.reshape(size * rows, columns)


def rows_major(matrix):
    return with_layout_constraint(matrix, Layout(major_to_minor=(0, 1)))


def after(value, *events):
    if value is None:
        return None
    return lax.optimization_barrier((value,) + events)[0]


def ring_shift(value, axis, step):
    size = lax.axis_size(axis)
    return lax.ppermute(value, axis, [(i, (i + step) % size) for i in range(size)])


def head_mask(rows, width, head_size, head):
    lane = lax.broadcasted_iota(jnp.int32, (rows, width), 1)
    return (lane // head_size == head).astype(f32)


def forward_kernel(live_ref, query_ref, *rest, head_size, blocks):
    key_refs, value_refs, out_ref = rest[:blocks], rest[blocks : 2 * blocks], rest[-1]
    rows, width = query_ref.shape
    column = lax.broadcasted_iota(jnp.int32, (1, blocks * rows), 1)
    usable = column < 0
    for i in range(blocks):
        usable = usable | ((column >= i * rows) & (column < i * rows + live_ref[i]))
    bias = jnp.where(usable, 0.0, negative)
    query = query_ref[...].astype(f32)
    keys = jnp.concatenate([ref[...] for ref in key_refs], axis=0)
    values = jnp.concatenate([ref[...] for ref in value_refs], axis=0)
    result = jnp.zeros((rows, width), f32)
    for head in range(width // head_size):
        mask = head_mask(rows, width, head_size, head)
        scores = dot((query * (mask * head_size ** (-0.5))).astype(bf16), keys, ((1,), (1,)))
        scores = scores + bias
        maximum = jnp.max(scores, axis=-1, keepdims=True)
        exponent = jnp.exp(scores - maximum)
        summed = jnp.sum(exponent, axis=-1, keepdims=True)
        attended = dot(exponent.astype(bf16), values, ((1,), (0,)))
        result = result + attended * (mask * (1.0 / summed))
    out_ref[...] = result.astype(bf16)


def backward_kernel(live_ref, query_ref, grad_ref, *rest, head_size, blocks):
    key_refs, value_refs = rest[:blocks], rest[blocks : 2 * blocks]
    query_grad_ref = rest[2 * blocks]
    grad_refs = rest[2 * blocks + 1 :]
    rows, width = query_ref.shape
    scaling = head_size ** (-0.5)
    key_position = lax.broadcasted_iota(jnp.int32, (rows, 1), 0)
    query_grad_ref[...] = jnp.zeros((rows, width), query_grad_ref.dtype)
    for ref in grad_refs:
        ref[...] = jnp.zeros((2, rows, width), ref.dtype)

    def one_head(head, carry):
        mask = head_mask(rows, width, head_size, head)
        query = query_ref[...].astype(f32)
        head_query = (query * mask).astype(bf16)
        scaled_query = (query * (mask * scaling)).astype(bf16)
        head_grads = (grad_ref[...].astype(f32) * mask).astype(bf16)
        scores = [
            jnp.where(
                key_position < live_ref[i],
                dot(key_refs[i][...], scaled_query, ((1,), (1,))),
                negative,
            )
            for i in range(blocks)
        ]
        maximum = scores[0].max(axis=0, keepdims=True)
        for item in scores[1:]:
            maximum = jnp.maximum(maximum, item.max(axis=0, keepdims=True))
        exponents = [jnp.exp(item - maximum) for item in scores]
        summed = sum(item.sum(axis=0, keepdims=True) for item in exponents)
        share = 1.0 / summed
        probabilities = [item * share for item in exponents]
        dprobs = [dot(value_refs[i][...], head_grads, ((1,), (1,))) for i in range(blocks)]
        row_total = sum(
            (p * d).sum(axis=0, keepdims=True) for p, d in zip(probabilities, dprobs)
        )
        query_grad = query_grad_ref[...].astype(f32)
        for i, ref in enumerate(grad_refs):
            value_grad = dot(probabilities[i].astype(bf16), head_grads, ((1,), (0,)))
            ref[1] = (ref[1].astype(f32) + value_grad).astype(ref.dtype)
            dscores = (probabilities[i] * (dprobs[i] - row_total) * scaling).astype(bf16)
            key_grad = dot(dscores, head_query, ((1,), (0,)))
            ref[0] = (ref[0].astype(f32) + key_grad).astype(ref.dtype)
            query_grad = query_grad + dot(dscores, key_refs[i][...], ((0,), (0,))) * mask
        query_grad_ref[...] = query_grad.astype(bf16)
        return carry

    lax.fori_loop(0, width // head_size, one_head, 0)


def column_block(rows, width, first):
    return pl.BlockSpec((rows, width), lambda p: (0, first + p))


def attend(live, query, own, others, head_size, interpret=False):
    rows, local = query.shape
    width = 2 * head_size
    pairs = local // width
    sources = [own] + list(others)
    blocks = len(sources)
    return pl.pallas_call(
        lambda *refs: forward_kernel(*refs, head_size=head_size, blocks=blocks),
        grid=(pairs,),
        in_specs=[pl.BlockSpec(memory_space=pltpu.SMEM), column_block(rows, width, 0)]
        + [column_block(rows, width, 0)] * blocks
        + [column_block(rows, width, pairs)] * blocks,
        out_specs=column_block(rows, width, 0),
        out_shape=jax.ShapeDtypeStruct((rows, local), bf16),
        cost_estimate=pl.CostEstimate(
            flops=4 * rows * rows * blocks * local,
            bytes_accessed=2 * rows * local * (2 + 2 * blocks),
            transcendentals=rows * rows * blocks * local // head_size,
        ),
        compiler_params=pltpu.CompilerParams(vmem_limit_bytes=56 * 1024 * 1024),
        name="attend",
        interpret=interpret,
    )(live, query, *sources, *sources)


def attend_back(live, query, grads, own, others, head_size, first, count, interpret=False):
    rows, full = query.shape
    width = 2 * head_size
    local = count * width
    pairs = full // width
    sources = [own] + list(others)
    blocks = len(sources)
    stacked = pl.BlockSpec((2, rows, width), lambda p: (0, 0, p))
    return pl.pallas_call(
        lambda *refs: backward_kernel(*refs, head_size=head_size, blocks=blocks),
        grid=(count,),
        in_specs=[pl.BlockSpec(memory_space=pltpu.SMEM)]
        + [column_block(rows, width, first)] * 2
        + [column_block(rows, width, first)] * blocks
        + [column_block(rows, width, pairs + first)] * blocks,
        out_specs=[column_block(rows, width, 0)] + [stacked] * blocks,
        out_shape=[
            jax.ShapeDtypeStruct((rows, local), bf16),
            jax.ShapeDtypeStruct((2, rows, local), f32),
        ]
        + [jax.ShapeDtypeStruct((2, rows, local), bf16)] * (blocks - 1),
        cost_estimate=pl.CostEstimate(
            flops=10 * rows * rows * blocks * local,
            bytes_accessed=2 * rows * local * (3 + 6 * blocks),
            transcendentals=rows * rows * blocks * local // head_size,
        ),
        compiler_params=pltpu.CompilerParams(vmem_limit_bytes=56 * 1024 * 1024),
        interpret=interpret,
    )(live, query, grads, *sources, *sources)


def body(
    inputs,
    lengths,
    first_gain,
    first_shift,
    qkv_weight,
    qkv_bias,
    proj_weight,
    proj_bias,
    attn_scale,
    second_gain,
    second_shift,
    up_weight,
    up_bias,
    down_weight,
    down_bias,
    mlp_scale,
    cotangent,
):
    images, slots, features = inputs.shape
    assert images == 1
    shards = lax.axis_size("fsdp")
    groups = lax.axis_size("ctx")
    place = lax.axis_index("ctx")
    width = qkv_weight.shape[2]
    inner = up_weight.shape[1]
    heads = qkv_bias.shape[1]
    head_size = qkv_bias.shape[2] * shards

    small = [
        first_gain,
        first_shift,
        qkv_bias,
        proj_bias,
        attn_scale,
        second_gain,
        second_shift,
        up_bias,
        down_bias,
        mlp_scale,
    ]
    sizes = [math.prod(item.shape) for item in small]
    packed = jnp.concatenate([item.reshape(-1) for item in small])
    gathered = lax.all_gather(packed, "fsdp", axis=0)
    full = []
    offset = 0
    for size in sizes:
        full.append(gathered[:, offset : offset + size].astype(f32))
        offset += size
    gain_one, shift_one, bias_pair, bias_proj, scale_one = full[:5]
    gain_two, shift_two, bias_up, bias_down, scale_two = full[5:]
    gain_one, shift_one, bias_proj, scale_one, gain_two, shift_two, bias_down, scale_two = [
        item.reshape(1, features)
        for item in (
            gain_one, shift_one, bias_proj, scale_one, gain_two, shift_two, bias_down, scale_two
        )
    ]
    bias_pair = (
        bias_pair.reshape(shards, 2, heads, -1).transpose(1, 2, 0, 3).reshape(2, width)
    )
    bias_up = bias_up.reshape(shards, up_bias.shape[0], -1).transpose(1, 0, 2).reshape(1, inner)

    qkv_matrix = lax.all_gather(
        qkv_weight.reshape(qkv_weight.shape[0], 3 * width), "fsdp", axis=0, tiled=True
    )
    proj_back = gather_by_permutes(proj_weight.T, "fsdp")
    piece = up_weight.shape[0] // groups
    up_piece = lax.dynamic_slice_in_dim(up_weight, place * piece, piece, 0)
    down_piece = lax.dynamic_slice_in_dim(down_weight, place * piece, piece, 1)
    mlp_full = lax.all_gather(
        jnp.concatenate([up_piece, down_piece.T], axis=1), ("fsdp", "ctx"), axis=0, tiled=True
    )
    up_full = mlp_full[:, :inner]
    down_back = mlp_full[:, inner:]

    source = inputs.reshape(slots, features).astype(f32)
    normed_one, unit_one, inverse_one = normalize(source, gain_one, shift_one)
    low_one = normed_one.astype(bf16)
    bias_kv = jnp.concatenate([jnp.zeros((width,), f32), bias_pair[1]])
    own = (dot(low_one, qkv_matrix[:, width:], ((1,), (0,))) + bias_kv).astype(bf16)
    others = [ring_shift(own, "ctx", step) for step in range(1, groups)]
    queries = (dot(low_one, qkv_matrix[:, :width], ((1,), (0,))) + bias_pair[0]).astype(bf16)
    order = (place - jnp.arange(groups, dtype=jnp.int32)) % groups
    live = jnp.take(lengths[0], order)
    mixed = attend(live, queries, own, others, head_size)

    proj_part = dot(mixed, proj_back, ((1,), (1,))).astype(bf16)
    projected = exchange_sum(proj_part, "tp") + bias_proj
    resid = source + scale_one * projected
    normed_two, unit_two, inverse_two = normalize(resid, gain_two, shift_two)
    low_two = normed_two.astype(bf16)
    hidden = dot(low_two, up_full, ((1,), (0,))) + bias_up
    cumulative, derivative = gelu_parts(hidden)
    activated = (hidden * cumulative).astype(bf16)

    row = lax.broadcasted_iota(jnp.int32, (slots, 1), 0)
    live_rows = (row < live[0]).astype(f32)
    upstream = cotangent.reshape(slots, features) * live_rows
    dmlp = upstream * scale_two
    grad_down_bias = jnp.sum(dmlp, axis=0)
    dmlp_low = dmlp.astype(bf16)
    dhidden = dot(dmlp_low, down_back, ((1,), (0,))) * derivative
    grad_up_bias = jnp.sum(dhidden, axis=0)
    dhidden_low = dhidden.astype(bf16)

    def reduce_shards(matrix):
        return lax.psum_scatter(matrix, "fsdp", scatter_dimension=0, tiled=True)

    up_part = dot(low_two, dhidden_low, ((0,), (0,))).astype(bf16)
    up_shard = reduce_shards(up_part)
    dnorm_part = dot(dhidden_low, up_full, ((1,), (1,))).astype(bf16)
    dnorm_other = swap_pair(dnorm_part, "tp")
    part = inner // groups
    if groups == 2:
        sent_units = lax.dynamic_slice_in_dim(activated, (1 - place) * part, part, 1)
        kept_units = lax.dynamic_slice_in_dim(activated, place * part, part, 1)
        down_sent = dot(dmlp_low, sent_units, ((0,), (0,))).astype(bf16)
        down_got = swap_pair(down_sent, "ctx")
        down_kept = dot(dmlp_low, kept_units, ((0,), (0,))).astype(bf16)
        down_kept = lax.optimization_barrier(down_kept)
        down_half = (down_kept.astype(f32) + down_got.astype(f32)).astype(bf16)
    else:
        down_half = lax.psum_scatter(
            dot(dmlp_low, activated, ((0,), (0,))).astype(bf16),
            "ctx",
            scatter_dimension=1,
            tiled=True,
        )
    down_part = dot(activated, down_back, ((1,), (1,))).astype(bf16)
    dnorm_two = pair_sum(dnorm_part, dnorm_other, "tp")
    mlp_other = swap_pair(down_part, "tp")

    grad_gain_two = jnp.sum(dnorm_two * unit_two, axis=0)
    grad_shift_two = jnp.sum(dnorm_two, axis=0)
    dresid = upstream + normalize_back(dnorm_two, unit_two, inverse_two, gain_two)
    grad_scale_one = jnp.sum(dresid * projected, axis=0)
    dproj = dresid * scale_one
    grad_proj_bias = jnp.sum(dproj, axis=0)
    dproj_low = dproj.astype(bf16)
    dmixed = dot(dproj_low, proj_back, ((1,), (0,))).astype(bf16)
    proj_grad_part = dot(dproj_low, mixed, ((0,), (0,))).astype(bf16)
    down_shard = rows_major(
        reduce_shards(rows_major(jnp.concatenate([down_half, proj_grad_part], axis=1)))
    )

    pairs = width // (2 * head_size)
    cuts = [0, pairs // 2, pairs] if pairs > 1 else [0, pairs]
    query_parts, own_parts = [], []
    for first, last in zip(cuts[:-1], cuts[1:]):
        query_piece, own_grad, *sent = attend_back(
            live, queries, dmixed, own, others, head_size, first, last - first
        )
        query_parts.append(query_piece)
        returned = [
            ring_shift(item, "ctx", -(step + 1)) for step, item in enumerate(sent)
        ]
        own_parts.append((own_grad, returned))
    mlp_other = after(mlp_other, query_parts[-1])
    mlp_out = pair_sum(down_part, mlp_other, "tp") + bias_down
    output = (resid + scale_two * mlp_out).astype(bf16).reshape(images, slots, features)
    grad_scale_two = jnp.sum(upstream * mlp_out, axis=0)
    totals = []
    for own_grad, returned in own_parts:
        for item in returned:
            own_grad = own_grad + item.astype(f32)
        totals.append(own_grad.astype(bf16))
    key_low = [item[0] for item in totals]
    value_low = [item[1] for item in totals]
    dqkv = jnp.concatenate(query_parts + key_low + value_low, axis=1)
    dnorm_local = dot(dqkv, qkv_matrix, ((1,), (1,)))
    grad_gain_one = jnp.sum(dnorm_local * unit_one, axis=0)
    grad_shift_one = jnp.sum(dnorm_local, axis=0)
    dnorm_low = dnorm_local.astype(bf16)
    dnorm_other = swap_pair(dnorm_low, "tp")
    dnorm_one = pair_sum(dnorm_low, dnorm_other, "tp")
    qkv_part = dot(low_one, dqkv, ((0,), (0,))).astype(bf16)
    qkv_shard = reduce_shards(qkv_part)
    up_other = swap_pair(up_shard, "ctx")
    grad_up = pair_sum(up_shard, up_other, "ctx")
    down_other = swap_pair(down_shard, "ctx")
    grad_proj = pair_sum(
        down_shard[:, part:], None if down_other is None else down_other[:, part:], "ctx"
    ).T
    if groups == 2:
        mine, yours = down_shard[:, :part], down_other[:, :part]
        grad_down = jnp.concatenate(
            [jnp.where(place == 0, mine, yours), jnp.where(place == 0, yours, mine)], axis=1
        )
    else:
        grad_down = lax.all_gather(down_shard[:, :part], "ctx", axis=1, tiled=True)
    grad_down = grad_down.astype(f32).T
    grad_qkv = exchange_sum(after(qkv_shard, grad_up, grad_down), "ctx")
    grad_qkv_bias = jnp.concatenate(
        [jnp.sum(item.astype(f32), axis=0) for item in query_parts + value_low]
    )
    dinput = (
        (dresid + normalize_back(dnorm_one, unit_one, inverse_one, gain_one))
        .astype(bf16)
        .reshape(images, slots, features)
    )

    pieces = [
        grad_gain_one,
        grad_shift_one,
        grad_qkv_bias.reshape(2, heads, shards, -1).transpose(2, 0, 1, 3),
        grad_proj_bias,
        grad_scale_one,
        grad_gain_two,
        grad_shift_two,
        grad_up_bias.reshape(up_bias.shape[0], shards, -1).transpose(1, 0, 2),
        grad_down_bias,
        grad_scale_two,
    ]
    sent_small = jnp.concatenate([item.reshape(shards, -1) for item in pieces], axis=1)
    got = lax.all_to_all(sent_small.astype(bf16), "fsdp", split_axis=0, concat_axis=0, tiled=True)
    total = jnp.sum(got.astype(f32), axis=0).astype(bf16)
    total = exchange_sum(total, "ctx")
    halves = sizes[0] + sizes[1]
    first_part = exchange_sum(total[:halves].astype(bf16), "tp")
    total = jnp.concatenate([first_part, total[halves:]])
    results = []
    offset = 0
    for item, size in zip(small, sizes):
        results.append(total[offset : offset + size].reshape(item.shape))
        offset += size
    (
        out_gain_one,
        out_shift_one,
        out_qkv_bias,
        out_proj_bias,
        out_scale_one,
        out_gain_two,
        out_shift_two,
        out_up_bias,
        out_down_bias,
        out_scale_two,
    ) = results
    return (
        output,
        dinput,
        out_gain_one,
        out_shift_one,
        grad_qkv.reshape(qkv_weight.shape),
        out_qkv_bias,
        grad_proj,
        out_proj_bias,
        out_scale_one,
        out_gain_two,
        out_shift_two,
        grad_up,
        out_up_bias,
        grad_down,
        out_down_bias,
        out_scale_two,
    )


def solution(mesh):
    rows = P("fsdp", "ctx", None)
    vector = P("fsdp")
    params = (
        vector,
        vector,
        P("fsdp", None, "tp"),
        P(None, "tp", "fsdp"),
        P("tp", "fsdp"),
        vector,
        vector,
        vector,
        vector,
        P("fsdp", "tp"),
        P("tp", "fsdp"),
        P("tp", "fsdp"),
        vector,
        vector,
    )

    return jax.shard_map(
        body,
        mesh=mesh,
        in_specs=(rows, P("fsdp", None)) + params + (rows,),
        out_specs=(rows, rows) + params,
        check_vma=False,
    )
```

```python
import math

import jax
import jax.numpy as jnp
from jax import lax
from jax.experimental import pallas as pl
from jax.experimental.pallas import tpu as pltpu
from jax.experimental.layout import Layout, with_layout_constraint
from jax.sharding import PartitionSpec as P


epsilon = 1e-06
negative = -1e30
f32 = jnp.float32
bf16 = jnp.bfloat16


def normalize(values, gain, shift):
    center = values - jnp.mean(values, axis=-1, keepdims=True)
    inverse = lax.rsqrt(jnp.mean(center * center, axis=-1, keepdims=True) + epsilon)
    standard = center * inverse
    return (standard * gain + shift, standard, inverse)


def normalize_back(upstream, standard, inverse, gain):
    scaled = upstream * gain
    return inverse * (
        scaled
        - jnp.mean(scaled, axis=-1, keepdims=True)
        - standard * jnp.mean(scaled * standard, axis=-1, keepdims=True)
    )


def gelu_parts(hidden):
    cumulative = 0.5 * (1.0 + jax.scipy.special.erf(hidden * (1.0 / math.sqrt(2.0))))
    density = jnp.exp(-0.5 * hidden * hidden) * (1.0 / math.sqrt(2.0 * math.pi))
    return (cumulative, cumulative + hidden * density)


def dot(left, right, dims):
    return lax.dot_general(left, right, (dims, ((), ())), preferred_element_type=f32)


def swap_pair(part, axis):
    if lax.axis_size(axis) == 2:
        return lax.ppermute(part, axis, [(0, 1), (1, 0)])
    return None


def pair_sum(part, other, axis):
    if other is None:
        return lax.psum(part, axis).astype(f32)
    return part.astype(f32) + other.astype(f32)


def exchange_sum(part, axis):
    return pair_sum(part, swap_pair(part, axis), axis)


def interleave_kernel(place_ref, same_ref, other_ref, out_ref, *, steps, rows):
    step, odd = place_ref[0], place_ref[1]
    for member in range(steps):
        piece = (step - member + steps) % steps
        mine, yours = same_ref[piece], other_ref[piece]
        first = 2 * member * rows
        out_ref[first : first + rows] = jnp.where(odd == 0, mine, yours)
        out_ref[first + rows : first + 2 * rows] = jnp.where(odd == 0, yours, mine)


def gather_by_permutes(shard, axis):
    size = lax.axis_size(axis)
    index = lax.axis_index(axis)
    steps = size // 2
    rows, columns = shard.shape
    pieces = [shard]
    for k in range(1, steps):
        pieces.append(
            lax.ppermute(shard, axis, [(i, (i + 2 * k) % size) for i in range(size)])
        )
    same = jnp.stack(pieces)
    other = lax.ppermute(same, axis, [(i, i ^ 1) for i in range(size)])
    whole = pl.BlockSpec((steps, rows, columns), lambda: (0, 0, 0))
    full = pl.pallas_call(
        lambda *refs: interleave_kernel(*refs, steps=steps, rows=rows),
        in_specs=[pl.BlockSpec(memory_space=pltpu.SMEM), whole, whole],
        out_specs=pl.BlockSpec((size * rows, columns), lambda: (0, 0)),
        out_shape=jax.ShapeDtypeStruct((size * rows, columns), shard.dtype),
    )(jnp.stack([index // 2, index % 2]).astype(jnp.int32), same, other)
    return full


def rows_major(matrix):
    return with_layout_constraint(matrix, Layout(major_to_minor=(0, 1)))


def after(value, *events):
    if value is None:
        return None
    return lax.optimization_barrier((value,) + events)[0]


def ring_shift(value, axis, step):
    size = lax.axis_size(axis)
    return lax.ppermute(value, axis, [(i, (i + step) % size) for i in range(size)])


def head_mask(rows, width, head_size, head):
    lane = lax.broadcasted_iota(jnp.int32, (rows, width), 1)
    return (lane // head_size == head).astype(f32)


def forward_kernel(live_ref, query_ref, *rest, head_size, blocks):
    key_refs, value_refs, out_ref = rest[:blocks], rest[blocks : 2 * blocks], rest[-1]
    rows, width = query_ref.shape
    column = lax.broadcasted_iota(jnp.int32, (1, blocks * rows), 1)
    usable = column < 0
    for i in range(blocks):
        usable = usable | ((column >= i * rows) & (column < i * rows + live_ref[i]))
    bias = jnp.where(usable, 0.0, negative)
    query = query_ref[...].astype(f32)
    keys = jnp.concatenate([ref[...] for ref in key_refs], axis=0)
    values = jnp.concatenate([ref[...] for ref in value_refs], axis=0)
    result = jnp.zeros((rows, width), f32)
    for head in range(width // head_size):
        mask = head_mask(rows, width, head_size, head)
        scores = dot((query * (mask * head_size ** (-0.5))).astype(bf16), keys, ((1,), (1,)))
        scores = scores + bias
        maximum = jnp.max(scores, axis=-1, keepdims=True)
        exponent = jnp.exp(scores - maximum)
        summed = jnp.sum(exponent, axis=-1, keepdims=True)
        attended = dot(exponent.astype(bf16), values, ((1,), (0,)))
        result = result + attended * (mask * (1.0 / summed))
    out_ref[...] = result.astype(bf16)


def backward_kernel(live_ref, query_ref, grad_ref, *rest, head_size, blocks):
    key_refs, value_refs = rest[:blocks], rest[blocks : 2 * blocks]
    query_grad_ref = rest[2 * blocks]
    grad_refs = rest[2 * blocks + 1 :]
    rows, width = query_ref.shape
    scaling = head_size ** (-0.5)
    key_position = lax.broadcasted_iota(jnp.int32, (rows, 1), 0)
    query_grad_ref[...] = jnp.zeros((rows, width), query_grad_ref.dtype)
    for ref in grad_refs:
        ref[...] = jnp.zeros((2, rows, width), ref.dtype)

    def one_head(head, carry):
        mask = head_mask(rows, width, head_size, head)
        query = query_ref[...].astype(f32)
        scaled_query = (query * (mask * scaling)).astype(bf16)
        head_grads = (grad_ref[...].astype(f32) * mask).astype(bf16)
        scores = [
            jnp.where(
                key_position < live_ref[i],
                dot(key_refs[i][...], scaled_query, ((1,), (1,))),
                negative,
            )
            for i in range(blocks)
        ]
        maximum = scores[0].max(axis=0, keepdims=True)
        for item in scores[1:]:
            maximum = jnp.maximum(maximum, item.max(axis=0, keepdims=True))
        exponents = [jnp.exp(item - maximum) for item in scores]
        summed = sum(item.sum(axis=0, keepdims=True) for item in exponents)
        share = 1.0 / summed
        probabilities = [item * share for item in exponents]
        dprobs = [dot(value_refs[i][...], head_grads, ((1,), (1,))) for i in range(blocks)]
        row_total = sum(
            (p * d).sum(axis=0, keepdims=True) for p, d in zip(probabilities, dprobs)
        )
        query_grad = query_grad_ref[...].astype(f32)
        for i, ref in enumerate(grad_refs):
            value_grad = dot(probabilities[i].astype(bf16), head_grads, ((1,), (0,)))
            ref[1] = (ref[1].astype(f32) + value_grad).astype(ref.dtype)
            dscores = (probabilities[i] * (dprobs[i] - row_total)).astype(bf16)
            key_grad = dot(dscores, scaled_query, ((1,), (0,)))
            ref[0] = (ref[0].astype(f32) + key_grad).astype(ref.dtype)
            query_grad = query_grad + dot(dscores, key_refs[i][...], ((0,), (0,))) * (
                mask * scaling
            )
        query_grad_ref[...] = query_grad.astype(bf16)
        return carry

    lax.fori_loop(0, width // head_size, one_head, 0)


def column_block(rows, width, first):
    return pl.BlockSpec((rows, width), lambda p: (0, first + p))


def attend(live, query, own, others, head_size, interpret=False):
    rows, local = query.shape
    width = 2 * head_size
    pairs = local // width
    sources = [own] + list(others)
    blocks = len(sources)
    return pl.pallas_call(
        lambda *refs: forward_kernel(*refs, head_size=head_size, blocks=blocks),
        grid=(pairs,),
        in_specs=[pl.BlockSpec(memory_space=pltpu.SMEM), column_block(rows, width, 0)]
        + [column_block(rows, width, 0)] * blocks
        + [column_block(rows, width, pairs)] * blocks,
        out_specs=column_block(rows, width, 0),
        out_shape=jax.ShapeDtypeStruct((rows, local), bf16),
        cost_estimate=pl.CostEstimate(
            flops=4 * rows * rows * blocks * local,
            bytes_accessed=2 * rows * local * (2 + 2 * blocks),
            transcendentals=rows * rows * blocks * local // head_size,
        ),
        compiler_params=pltpu.CompilerParams(vmem_limit_bytes=56 * 1024 * 1024),
        name="attend",
        interpret=interpret,
    )(live, query, *sources, *sources)


def attend_back(live, query, grads, own, others, head_size, first, count, interpret=False):
    rows, full = query.shape
    width = 2 * head_size
    local = count * width
    pairs = full // width
    sources = [own] + list(others)
    blocks = len(sources)
    stacked = pl.BlockSpec((2, rows, width), lambda p: (0, 0, p))
    return pl.pallas_call(
        lambda *refs: backward_kernel(*refs, head_size=head_size, blocks=blocks),
        grid=(count,),
        in_specs=[pl.BlockSpec(memory_space=pltpu.SMEM)]
        + [column_block(rows, width, first)] * 2
        + [column_block(rows, width, first)] * blocks
        + [column_block(rows, width, pairs + first)] * blocks,
        out_specs=[column_block(rows, width, 0)] + [stacked] * blocks,
        out_shape=[
            jax.ShapeDtypeStruct((rows, local), bf16),
            jax.ShapeDtypeStruct((2, rows, local), f32),
        ]
        + [jax.ShapeDtypeStruct((2, rows, local), bf16)] * (blocks - 1),
        cost_estimate=pl.CostEstimate(
            flops=10 * rows * rows * blocks * local,
            bytes_accessed=2 * rows * local * (3 + 6 * blocks),
            transcendentals=rows * rows * blocks * local // head_size,
        ),
        compiler_params=pltpu.CompilerParams(vmem_limit_bytes=56 * 1024 * 1024),
        interpret=interpret,
    )(live, query, grads, *sources, *sources)


def body(
    inputs,
    lengths,
    first_gain,
    first_shift,
    qkv_weight,
    qkv_bias,
    proj_weight,
    proj_bias,
    attn_scale,
    second_gain,
    second_shift,
    up_weight,
    up_bias,
    down_weight,
    down_bias,
    mlp_scale,
    cotangent,
):
    images, slots, features = inputs.shape
    assert images == 1
    shards = lax.axis_size("fsdp")
    groups = lax.axis_size("ctx")
    place = lax.axis_index("ctx")
    width = qkv_weight.shape[2]
    inner = up_weight.shape[1]
    heads = qkv_bias.shape[1]
    head_size = qkv_bias.shape[2] * shards

    small = [
        first_gain,
        first_shift,
        qkv_bias,
        proj_bias,
        attn_scale,
        second_gain,
        second_shift,
        up_bias,
        down_bias,
        mlp_scale,
    ]
    sizes = [math.prod(item.shape) for item in small]
    base = first_gain.shape[0]
    packed = jnp.concatenate([item.reshape(-1, base) for item in small], axis=0)
    gathered = lax.all_gather(packed, "fsdp", axis=0).reshape(shards, -1)
    full = []
    offset = 0
    for size in sizes:
        full.append(gathered[:, offset : offset + size].astype(f32))
        offset += size
    gain_one, shift_one, bias_pair, bias_proj, scale_one = full[:5]
    gain_two, shift_two, bias_up, bias_down, scale_two = full[5:]
    gain_one, shift_one, bias_proj, scale_one, gain_two, shift_two, bias_down, scale_two = [
        item.reshape(1, features)
        for item in (
            gain_one, shift_one, bias_proj, scale_one, gain_two, shift_two, bias_down, scale_two
        )
    ]
    bias_pair = (
        bias_pair.reshape(shards, 2, heads, -1).transpose(1, 2, 0, 3).reshape(2, width)
    )
    bias_up = bias_up.reshape(shards, up_bias.shape[0], -1).transpose(1, 0, 2).reshape(1, inner)

    kv_full = lax.all_gather(
        qkv_weight[:, 1:].reshape(qkv_weight.shape[0], 2 * width), "fsdp", axis=0, tiled=True
    )
    query_full = gather_by_permutes(qkv_weight[:, 0], "fsdp")
    proj_back = gather_by_permutes(proj_weight.T, "fsdp")
    piece = up_weight.shape[0] // groups
    up_piece = lax.dynamic_slice_in_dim(up_weight, place * piece, piece, 0)
    down_piece = lax.dynamic_slice_in_dim(down_weight, place * piece, piece, 1)
    mlp_full = lax.all_gather(
        jnp.concatenate([up_piece, down_piece.T], axis=1), ("fsdp", "ctx"), axis=0, tiled=True
    )
    up_full = mlp_full[:, :inner]
    down_back = mlp_full[:, inner:]

    source = inputs.reshape(slots, features).astype(f32)
    normed_one, unit_one, inverse_one = normalize(source, gain_one, shift_one)
    low_one = normed_one.astype(bf16)
    bias_kv = jnp.concatenate([jnp.zeros((width,), f32), bias_pair[1]])
    own = (dot(low_one, kv_full, ((1,), (0,))) + bias_kv).astype(bf16)
    others = [ring_shift(own, "ctx", step) for step in range(1, groups)]
    queries = (dot(low_one, query_full, ((1,), (0,))) + bias_pair[0]).astype(bf16)
    order = (place - jnp.arange(groups, dtype=jnp.int32)) % groups
    live = jnp.take(lengths[0], order)
    mixed = attend(live, queries, own, others, head_size)

    proj_part = dot(mixed, proj_back, ((1,), (1,))).astype(bf16)
    proj_other = swap_pair(proj_part, "tp")
    qkv_matrix = jnp.concatenate([query_full, kv_full], axis=1)
    projected = pair_sum(proj_part, proj_other, "tp") + bias_proj
    resid = source + scale_one * projected
    normed_two, unit_two, inverse_two = normalize(resid, gain_two, shift_two)
    low_two = normed_two.astype(bf16)
    hidden = dot(low_two, up_full, ((1,), (0,))) + bias_up
    cumulative, derivative = gelu_parts(hidden)
    activated = (hidden * cumulative).astype(bf16)

    row = lax.broadcasted_iota(jnp.int32, (slots, 1), 0)
    live_rows = (row < live[0]).astype(f32)
    upstream = cotangent.reshape(slots, features) * live_rows
    dmlp = upstream * scale_two
    grad_down_bias = jnp.sum(dmlp, axis=0)
    dmlp_low = dmlp.astype(bf16)
    dhidden = dot(dmlp_low, down_back, ((1,), (0,))) * derivative
    grad_up_bias = jnp.sum(dhidden, axis=0)
    dhidden_low = dhidden.astype(bf16)

    def reduce_shards(matrix):
        return lax.psum_scatter(matrix, "fsdp", scatter_dimension=0, tiled=True)

    up_part = dot(low_two, dhidden_low, ((0,), (0,))).astype(bf16)
    up_shard = reduce_shards(up_part)
    dnorm_part = dot(dhidden_low, up_full, ((1,), (1,))).astype(bf16)
    dnorm_other = swap_pair(dnorm_part, "tp")
    part = inner // groups
    if groups == 2:
        sent_units = lax.dynamic_slice_in_dim(activated, (1 - place) * part, part, 1)
        kept_units = lax.dynamic_slice_in_dim(activated, place * part, part, 1)
        down_sent = dot(dmlp_low, sent_units, ((0,), (0,))).astype(bf16)
        down_got = swap_pair(down_sent, "ctx")
        down_kept = dot(dmlp_low, kept_units, ((0,), (0,))).astype(bf16)
        down_kept = lax.optimization_barrier(down_kept)
        down_half = (down_kept.astype(f32) + down_got.astype(f32)).astype(bf16)
    else:
        down_half = lax.psum_scatter(
            dot(dmlp_low, activated, ((0,), (0,))).astype(bf16),
            "ctx",
            scatter_dimension=1,
            tiled=True,
        )
    down_part = dot(activated, down_back, ((1,), (1,))).astype(bf16)
    dnorm_two = pair_sum(dnorm_part, dnorm_other, "tp")
    mlp_other = swap_pair(down_part, "tp")

    grad_gain_two = jnp.sum(dnorm_two * unit_two, axis=0)
    grad_shift_two = jnp.sum(dnorm_two, axis=0)
    dresid = upstream + normalize_back(dnorm_two, unit_two, inverse_two, gain_two)
    grad_scale_one = jnp.sum(dresid * projected, axis=0)
    dproj = dresid * scale_one
    grad_proj_bias = jnp.sum(dproj, axis=0)
    dproj_low = dproj.astype(bf16)
    dmixed = dot(dproj_low, proj_back, ((1,), (0,))).astype(bf16)
    proj_grad_part = dot(dproj_low, mixed, ((0,), (0,))).astype(bf16)
    down_shard = rows_major(
        reduce_shards(rows_major(jnp.concatenate([down_half, proj_grad_part], axis=1)))
    )

    pairs = width // (2 * head_size)
    cuts = [0, pairs // 2, pairs] if pairs > 1 else [0, pairs]
    query_parts, own_parts = [], []
    for first, last in zip(cuts[:-1], cuts[1:]):
        query_piece, own_grad, *sent = attend_back(
            live, queries, dmixed, own, others, head_size, first, last - first
        )
        query_parts.append(query_piece)
        returned = [
            ring_shift(item, "ctx", -(step + 1)) for step, item in enumerate(sent)
        ]
        own_parts.append((own_grad, returned))
    mlp_other = after(mlp_other, query_parts[-1])
    mlp_out = pair_sum(down_part, mlp_other, "tp") + bias_down
    output = (resid + scale_two * mlp_out).astype(bf16).reshape(images, slots, features)
    grad_scale_two = jnp.sum(upstream * mlp_out, axis=0)
    totals = []
    for own_grad, returned in own_parts:
        for item in returned:
            own_grad = own_grad + item.astype(f32)
        totals.append(own_grad.astype(bf16))
    key_low = [item[0] for item in totals]
    value_low = [item[1] for item in totals]
    dqkv = jnp.concatenate(query_parts + key_low + value_low, axis=1)
    dnorm_local = dot(dqkv, qkv_matrix, ((1,), (1,)))
    grad_gain_one = jnp.sum(dnorm_local * unit_one, axis=0)
    grad_shift_one = jnp.sum(dnorm_local, axis=0)
    dnorm_low = dnorm_local.astype(bf16)
    dnorm_other = swap_pair(dnorm_low, "tp")
    dnorm_one = pair_sum(dnorm_low, dnorm_other, "tp")
    qkv_part = dot(low_one, dqkv, ((0,), (0,))).astype(bf16)
    qkv_shard = reduce_shards(qkv_part)
    up_other = swap_pair(up_shard, "ctx")
    grad_up = pair_sum(up_shard, up_other, "ctx")
    down_other = swap_pair(down_shard, "ctx")
    grad_proj = pair_sum(
        down_shard[:, part:], None if down_other is None else down_other[:, part:], "ctx"
    ).T
    if groups == 2:
        mine, yours = down_shard[:, :part], down_other[:, :part]
        grad_down = jnp.concatenate(
            [jnp.where(place == 0, mine, yours), jnp.where(place == 0, yours, mine)], axis=1
        )
    else:
        grad_down = lax.all_gather(down_shard[:, :part], "ctx", axis=1, tiled=True)
    grad_down = grad_down.astype(f32).T
    grad_qkv = exchange_sum(after(qkv_shard, grad_up, grad_down), "ctx")
    grad_qkv_bias = jnp.concatenate(
        [jnp.sum(item.astype(f32), axis=0) for item in query_parts + value_low]
    )
    dinput = (
        (dresid + normalize_back(dnorm_one, unit_one, inverse_one, gain_one))
        .astype(bf16)
        .reshape(images, slots, features)
    )

    pieces = [
        grad_gain_one,
        grad_shift_one,
        grad_qkv_bias.reshape(2, heads, shards, -1).transpose(2, 0, 1, 3),
        grad_proj_bias,
        grad_scale_one,
        grad_gain_two,
        grad_shift_two,
        grad_up_bias.reshape(up_bias.shape[0], shards, -1).transpose(1, 0, 2),
        grad_down_bias,
        grad_scale_two,
    ]
    sent_small = jnp.concatenate([item.reshape(shards, -1) for item in pieces], axis=1)
    got = lax.all_to_all(sent_small.astype(bf16), "fsdp", split_axis=0, concat_axis=0, tiled=True)
    total = jnp.sum(got.astype(f32), axis=0).astype(bf16)
    total = exchange_sum(total, "ctx")
    halves = sizes[0] + sizes[1]
    first_part = exchange_sum(total[:halves].astype(bf16), "tp")
    total = jnp.concatenate([first_part, total[halves:]])
    results = []
    offset = 0
    for item, size in zip(small, sizes):
        results.append(total[offset : offset + size].reshape(item.shape))
        offset += size
    (
        out_gain_one,
        out_shift_one,
        out_qkv_bias,
        out_proj_bias,
        out_scale_one,
        out_gain_two,
        out_shift_two,
        out_up_bias,
        out_down_bias,
        out_scale_two,
    ) = results
    return (
        output,
        dinput,
        out_gain_one,
        out_shift_one,
        grad_qkv.reshape(qkv_weight.shape),
        out_qkv_bias,
        grad_proj,
        out_proj_bias,
        out_scale_one,
        out_gain_two,
        out_shift_two,
        grad_up,
        out_up_bias,
        grad_down,
        out_down_bias,
        out_scale_two,
    )


def solution(mesh):
    rows = P("fsdp", "ctx", None)
    vector = P("fsdp")
    params = (
        vector,
        vector,
        P("fsdp", None, "tp"),
        P(None, "tp", "fsdp"),
        P("tp", "fsdp"),
        vector,
        vector,
        vector,
        vector,
        P("fsdp", "tp"),
        P("tp", "fsdp"),
        P("tp", "fsdp"),
        vector,
        vector,
    )

    return jax.shard_map(
        body,
        mesh=mesh,
        in_specs=(rows, P("fsdp", None)) + params + (rows,),
        out_specs=(rows, rows) + params,
        check_vma=False,
    )
```

```python
import math

import jax
import jax.numpy as jnp
from jax import lax
from jax.experimental import pallas as pl
from jax.experimental.pallas import tpu as pltpu
from jax.experimental.layout import Layout, with_layout_constraint
from jax.sharding import PartitionSpec as P


epsilon = 1e-06
negative = -1e30
f32 = jnp.float32
bf16 = jnp.bfloat16


def normalize(values, gain, shift):
    center = values - jnp.mean(values, axis=-1, keepdims=True)
    inverse = lax.rsqrt(jnp.mean(center * center, axis=-1, keepdims=True) + epsilon)
    standard = center * inverse
    return (standard * gain + shift, standard, inverse)


def normalize_back(upstream, standard, inverse, gain):
    scaled = upstream * gain
    return inverse * (
        scaled
        - jnp.mean(scaled, axis=-1, keepdims=True)
        - standard * jnp.mean(scaled * standard, axis=-1, keepdims=True)
    )


def gelu_parts(hidden):
    cumulative = 0.5 * (1.0 + jax.scipy.special.erf(hidden * (1.0 / math.sqrt(2.0))))
    density = jnp.exp(-0.5 * hidden * hidden) * (1.0 / math.sqrt(2.0 * math.pi))
    return (cumulative, cumulative + hidden * density)


def dot(left, right, dims):
    return lax.dot_general(left, right, (dims, ((), ())), preferred_element_type=f32)


def swap_pair(part, axis):
    if lax.axis_size(axis) == 2:
        return lax.ppermute(part, axis, [(0, 1), (1, 0)])
    return None


def pair_sum(part, other, axis):
    if other is None:
        return lax.psum(part, axis).astype(f32)
    return part.astype(f32) + other.astype(f32)


def exchange_sum(part, axis):
    return pair_sum(part, swap_pair(part, axis), axis)


def gather_by_permutes(shard, axis):
    size = lax.axis_size(axis)
    index = lax.axis_index(axis)
    steps = size // 2
    rows, columns = shard.shape
    pieces = [shard]
    for k in range(1, steps):
        pieces.append(
            lax.ppermute(shard, axis, [(i, (i + 2 * k) % size) for i in range(size)])
        )
    backward = jnp.concatenate(pieces[::-1] * 2, axis=0)
    start = (steps - 1 - index // 2) * rows
    same = lax.dynamic_slice_in_dim(backward, start, steps * rows, 0)
    other = lax.ppermute(same, axis, [(i, i ^ 1) for i in range(size)])
    same = same.reshape(steps, 1, rows, columns)
    other = other.reshape(steps, 1, rows, columns)
    even = (index % 2 == 0) == (
        lax.broadcasted_iota(jnp.int32, (1, 2, 1, 1), 1) == 0
    )
    full = jnp.where(even, same, other)
    return full.reshape(size * rows, columns)


def rows_major(matrix):
    return with_layout_constraint(matrix, Layout(major_to_minor=(0, 1)))


def after(value, *events):
    if value is None:
        return None
    return lax.optimization_barrier((value,) + events)[0]


def ring_shift(value, axis, step):
    size = lax.axis_size(axis)
    return lax.ppermute(value, axis, [(i, (i + step) % size) for i in range(size)])


def head_mask(rows, width, head_size, head):
    lane = lax.broadcasted_iota(jnp.int32, (rows, width), 1)
    return (lane // head_size == head).astype(f32)


def forward_kernel(live_ref, query_ref, *rest, head_size, blocks):
    key_refs, value_refs, out_ref = rest[:blocks], rest[blocks : 2 * blocks], rest[-1]
    rows, width = query_ref.shape
    column = lax.broadcasted_iota(jnp.int32, (1, blocks * rows), 1)
    usable = column < 0
    for i in range(blocks):
        usable = usable | ((column >= i * rows) & (column < i * rows + live_ref[i]))
    bias = jnp.where(usable, 0.0, negative)
    query = query_ref[...].astype(f32)
    keys = jnp.concatenate([ref[...] for ref in key_refs], axis=0)
    values = jnp.concatenate([ref[...] for ref in value_refs], axis=0)
    result = jnp.zeros((rows, width), f32)
    for head in range(width // head_size):
        mask = head_mask(rows, width, head_size, head)
        scores = dot((query * (mask * head_size ** (-0.5))).astype(bf16), keys, ((1,), (1,)))
        scores = scores + bias
        maximum = jnp.max(scores, axis=-1, keepdims=True)
        exponent = jnp.exp(scores - maximum)
        summed = jnp.sum(exponent, axis=-1, keepdims=True)
        attended = dot(exponent.astype(bf16), values, ((1,), (0,)))
        result = result + attended * (mask * (1.0 / summed))
    out_ref[...] = result.astype(bf16)


def backward_kernel(live_ref, query_ref, grad_ref, *rest, head_size, blocks):
    key_refs, value_refs = rest[:blocks], rest[blocks : 2 * blocks]
    query_grad_ref = rest[2 * blocks]
    grad_refs = rest[2 * blocks + 1 :]
    rows, width = query_ref.shape
    scaling = head_size ** (-0.5)
    key_position = lax.broadcasted_iota(jnp.int32, (rows, 1), 0)
    query_grad_ref[...] = jnp.zeros((rows, width), query_grad_ref.dtype)
    for ref in grad_refs:
        ref[...] = jnp.zeros((2, rows, width), ref.dtype)

    def one_head(head, carry):
        mask = head_mask(rows, width, head_size, head)
        query = query_ref[...].astype(f32)
        scaled_query = (query * (mask * scaling)).astype(bf16)
        head_grads = (grad_ref[...].astype(f32) * mask).astype(bf16)
        scores = [
            jnp.where(
                key_position < live_ref[i],
                dot(key_refs[i][...], scaled_query, ((1,), (1,))),
                negative,
            )
            for i in range(blocks)
        ]
        maximum = scores[0].max(axis=0, keepdims=True)
        for item in scores[1:]:
            maximum = jnp.maximum(maximum, item.max(axis=0, keepdims=True))
        exponents = [jnp.exp(item - maximum) for item in scores]
        summed = sum(item.sum(axis=0, keepdims=True) for item in exponents)
        share = 1.0 / summed
        probabilities = [item * share for item in exponents]
        dprobs = [dot(value_refs[i][...], head_grads, ((1,), (1,))) for i in range(blocks)]
        row_total = sum(
            (p * d).sum(axis=0, keepdims=True) for p, d in zip(probabilities, dprobs)
        )
        query_grad = query_grad_ref[...].astype(f32)
        for i, ref in enumerate(grad_refs):
            value_grad = dot(probabilities[i].astype(bf16), head_grads, ((1,), (0,)))
            ref[1] = (ref[1].astype(f32) + value_grad).astype(ref.dtype)
            dscores = (probabilities[i] * (dprobs[i] - row_total)).astype(bf16)
            key_grad = dot(dscores, scaled_query, ((1,), (0,)))
            ref[0] = (ref[0].astype(f32) + key_grad).astype(ref.dtype)
            query_grad = query_grad + dot(dscores, key_refs[i][...], ((0,), (0,))) * (
                mask * scaling
            )
        query_grad_ref[...] = query_grad.astype(bf16)
        return carry

    lax.fori_loop(0, width // head_size, one_head, 0)


def column_block(rows, width, first):
    return pl.BlockSpec((rows, width), lambda p: (0, first + p))


def attend(live, query, own, others, head_size, interpret=False):
    rows, local = query.shape
    width = 2 * head_size
    pairs = local // width
    sources = [own] + list(others)
    blocks = len(sources)
    return pl.pallas_call(
        lambda *refs: forward_kernel(*refs, head_size=head_size, blocks=blocks),
        grid=(pairs,),
        in_specs=[pl.BlockSpec(memory_space=pltpu.SMEM), column_block(rows, width, 0)]
        + [column_block(rows, width, 0)] * blocks
        + [column_block(rows, width, pairs)] * blocks,
        out_specs=column_block(rows, width, 0),
        out_shape=jax.ShapeDtypeStruct((rows, local), bf16),
        cost_estimate=pl.CostEstimate(
            flops=4 * rows * rows * blocks * local,
            bytes_accessed=2 * rows * local * (2 + 2 * blocks),
            transcendentals=rows * rows * blocks * local // head_size,
        ),
        compiler_params=pltpu.CompilerParams(vmem_limit_bytes=56 * 1024 * 1024),
        name="attend",
        interpret=interpret,
    )(live, query, *sources, *sources)


def attend_back(live, query, grads, own, others, head_size, first, count, interpret=False):
    rows, full = query.shape
    width = 2 * head_size
    local = count * width
    pairs = full // width
    sources = [own] + list(others)
    blocks = len(sources)
    stacked = pl.BlockSpec((2, rows, width), lambda p: (0, 0, p))
    return pl.pallas_call(
        lambda *refs: backward_kernel(*refs, head_size=head_size, blocks=blocks),
        grid=(count,),
        in_specs=[pl.BlockSpec(memory_space=pltpu.SMEM)]
        + [column_block(rows, width, first)] * 2
        + [column_block(rows, width, first)] * blocks
        + [column_block(rows, width, pairs + first)] * blocks,
        out_specs=[column_block(rows, width, 0)] + [stacked] * blocks,
        out_shape=[
            jax.ShapeDtypeStruct((rows, local), bf16),
            jax.ShapeDtypeStruct((2, rows, local), f32),
        ]
        + [jax.ShapeDtypeStruct((2, rows, local), bf16)] * (blocks - 1),
        cost_estimate=pl.CostEstimate(
            flops=10 * rows * rows * blocks * local,
            bytes_accessed=2 * rows * local * (3 + 6 * blocks),
            transcendentals=rows * rows * blocks * local // head_size,
        ),
        compiler_params=pltpu.CompilerParams(vmem_limit_bytes=56 * 1024 * 1024),
        interpret=interpret,
    )(live, query, grads, *sources, *sources)


def body(
    inputs,
    lengths,
    first_gain,
    first_shift,
    qkv_weight,
    qkv_bias,
    proj_weight,
    proj_bias,
    attn_scale,
    second_gain,
    second_shift,
    up_weight,
    up_bias,
    down_weight,
    down_bias,
    mlp_scale,
    cotangent,
):
    images, slots, features = inputs.shape
    assert images == 1
    shards = lax.axis_size("fsdp")
    groups = lax.axis_size("ctx")
    place = lax.axis_index("ctx")
    width = qkv_weight.shape[2]
    inner = up_weight.shape[1]
    heads = qkv_bias.shape[1]
    head_size = qkv_bias.shape[2] * shards

    small = [
        first_gain,
        first_shift,
        qkv_bias,
        proj_bias,
        attn_scale,
        second_gain,
        second_shift,
        up_bias,
        down_bias,
        mlp_scale,
    ]
    sizes = [math.prod(item.shape) for item in small]
    base = first_gain.shape[0]
    packed = jnp.concatenate([item.reshape(-1, base) for item in small], axis=0)
    gathered = lax.all_gather(packed, "fsdp", axis=0).reshape(shards, -1)
    full = []
    offset = 0
    for size in sizes:
        full.append(gathered[:, offset : offset + size].astype(f32))
        offset += size
    gain_one, shift_one, bias_pair, bias_proj, scale_one = full[:5]
    gain_two, shift_two, bias_up, bias_down, scale_two = full[5:]
    gain_one, shift_one, bias_proj, scale_one, gain_two, shift_two, bias_down, scale_two = [
        item.reshape(1, features)
        for item in (
            gain_one, shift_one, bias_proj, scale_one, gain_two, shift_two, bias_down, scale_two
        )
    ]
    bias_pair = (
        bias_pair.reshape(shards, 2, heads, -1).transpose(1, 2, 0, 3).reshape(2, width)
    )
    bias_up = bias_up.reshape(shards, up_bias.shape[0], -1).transpose(1, 0, 2).reshape(1, inner)

    qkv_matrix = lax.all_gather(
        qkv_weight.reshape(qkv_weight.shape[0], 3 * width), "fsdp", axis=0, tiled=True
    )
    proj_back = gather_by_permutes(proj_weight.T, "fsdp")
    piece = up_weight.shape[0] // groups
    up_piece = lax.dynamic_slice_in_dim(up_weight, place * piece, piece, 0)
    down_piece = lax.dynamic_slice_in_dim(down_weight, place * piece, piece, 1)
    mlp_full = lax.all_gather(
        jnp.concatenate([up_piece, down_piece.T], axis=1), ("fsdp", "ctx"), axis=0, tiled=True
    )
    up_full = mlp_full[:, :inner]
    down_back = mlp_full[:, inner:]

    source = inputs.reshape(slots, features).astype(f32)
    normed_one, unit_one, inverse_one = normalize(source, gain_one, shift_one)
    low_one = normed_one.astype(bf16)
    bias_kv = jnp.concatenate([jnp.zeros((width,), f32), bias_pair[1]])
    own = (dot(low_one, qkv_matrix[:, width:], ((1,), (0,))) + bias_kv).astype(bf16)
    others = [ring_shift(own, "ctx", step) for step in range(1, groups)]
    queries = (dot(low_one, qkv_matrix[:, :width], ((1,), (0,))) + bias_pair[0]).astype(bf16)
    order = (place - jnp.arange(groups, dtype=jnp.int32)) % groups
    live = jnp.take(lengths[0], order)
    mixed = attend(live, queries, own, others, head_size)

    proj_part = dot(mixed, proj_back, ((1,), (1,))).astype(bf16)
    projected = exchange_sum(proj_part, "tp") + bias_proj
    resid = source + scale_one * projected
    normed_two, unit_two, inverse_two = normalize(resid, gain_two, shift_two)
    low_two = normed_two.astype(bf16)
    hidden = dot(low_two, up_full, ((1,), (0,))) + bias_up
    cumulative, derivative = gelu_parts(hidden)
    activated = (hidden * cumulative).astype(bf16)

    row = lax.broadcasted_iota(jnp.int32, (slots, 1), 0)
    live_rows = (row < live[0]).astype(f32)
    upstream = cotangent.reshape(slots, features) * live_rows
    dmlp = upstream * scale_two
    grad_down_bias = jnp.sum(dmlp, axis=0)
    dmlp_low = dmlp.astype(bf16)
    dhidden = dot(dmlp_low, down_back, ((1,), (0,))) * derivative
    grad_up_bias = jnp.sum(dhidden, axis=0)
    dhidden_low = dhidden.astype(bf16)

    def reduce_shards(matrix):
        return lax.psum_scatter(matrix, "fsdp", scatter_dimension=0, tiled=True)

    up_part = dot(low_two, dhidden_low, ((0,), (0,))).astype(bf16)
    up_shard = reduce_shards(up_part)
    dnorm_part = dot(dhidden_low, up_full, ((1,), (1,))).astype(bf16)
    dnorm_other = swap_pair(dnorm_part, "tp")
    part = inner // groups
    if groups == 2:
        sent_units = lax.dynamic_slice_in_dim(activated, (1 - place) * part, part, 1)
        kept_units = lax.dynamic_slice_in_dim(activated, place * part, part, 1)
        down_sent = dot(dmlp_low, sent_units, ((0,), (0,))).astype(bf16)
        down_got = swap_pair(down_sent, "ctx")
        down_kept = dot(dmlp_low, kept_units, ((0,), (0,))).astype(bf16)
        down_kept = lax.optimization_barrier(down_kept)
        down_half = (down_kept.astype(f32) + down_got.astype(f32)).astype(bf16)
    else:
        down_half = lax.psum_scatter(
            dot(dmlp_low, activated, ((0,), (0,))).astype(bf16),
            "ctx",
            scatter_dimension=1,
            tiled=True,
        )
    down_part = dot(activated, down_back, ((1,), (1,))).astype(bf16)
    dnorm_two = pair_sum(dnorm_part, dnorm_other, "tp")
    mlp_other = swap_pair(down_part, "tp")

    grad_gain_two = jnp.sum(dnorm_two * unit_two, axis=0)
    grad_shift_two = jnp.sum(dnorm_two, axis=0)
    dresid = upstream + normalize_back(dnorm_two, unit_two, inverse_two, gain_two)
    grad_scale_one = jnp.sum(dresid * projected, axis=0)
    dproj = dresid * scale_one
    grad_proj_bias = jnp.sum(dproj, axis=0)
    dproj_low = dproj.astype(bf16)
    dmixed = dot(dproj_low, proj_back, ((1,), (0,))).astype(bf16)
    proj_grad_part = dot(dproj_low, mixed, ((0,), (0,))).astype(bf16)
    down_shard = rows_major(
        reduce_shards(rows_major(jnp.concatenate([down_half, proj_grad_part], axis=1)))
    )

    pairs = width // (2 * head_size)
    cuts = [0, pairs // 2, pairs] if pairs > 1 else [0, pairs]
    query_parts, own_parts = [], []
    for first, last in zip(cuts[:-1], cuts[1:]):
        query_piece, own_grad, *sent = attend_back(
            live, queries, dmixed, own, others, head_size, first, last - first
        )
        query_parts.append(query_piece)
        returned = [
            ring_shift(item, "ctx", -(step + 1)) for step, item in enumerate(sent)
        ]
        own_parts.append((own_grad, returned))
    mlp_other = after(mlp_other, query_parts[-1])
    mlp_out = pair_sum(down_part, mlp_other, "tp") + bias_down
    output = (resid + scale_two * mlp_out).astype(bf16).reshape(images, slots, features)
    grad_scale_two = jnp.sum(upstream * mlp_out, axis=0)
    totals = []
    for own_grad, returned in own_parts:
        for item in returned:
            own_grad = own_grad + item.astype(f32)
        totals.append(own_grad.astype(bf16))
    key_low = [item[0] for item in totals]
    value_low = [item[1] for item in totals]
    dqkv = jnp.concatenate(query_parts + key_low + value_low, axis=1)
    dnorm_local = dot(dqkv, qkv_matrix, ((1,), (1,)))
    grad_gain_one = jnp.sum(dnorm_local * unit_one, axis=0)
    grad_shift_one = jnp.sum(dnorm_local, axis=0)
    dnorm_low = dnorm_local.astype(bf16)
    dnorm_other = swap_pair(dnorm_low, "tp")
    dnorm_one = pair_sum(dnorm_low, dnorm_other, "tp")
    qkv_part = dot(low_one, dqkv, ((0,), (0,))).astype(bf16)
    qkv_shard = reduce_shards(qkv_part)
    up_other = swap_pair(up_shard, "ctx")
    grad_up = pair_sum(up_shard, up_other, "ctx")
    down_other = swap_pair(down_shard, "ctx")
    grad_proj = pair_sum(
        down_shard[:, part:], None if down_other is None else down_other[:, part:], "ctx"
    ).T
    if groups == 2:
        mine, yours = down_shard[:, :part], down_other[:, :part]
        grad_down = jnp.concatenate(
            [jnp.where(place == 0, mine, yours), jnp.where(place == 0, yours, mine)], axis=1
        )
    else:
        grad_down = lax.all_gather(down_shard[:, :part], "ctx", axis=1, tiled=True)
    grad_down = grad_down.astype(f32).T
    grad_qkv = exchange_sum(after(qkv_shard, grad_up, grad_down), "ctx")
    grad_qkv_bias = jnp.concatenate(
        [jnp.sum(item.astype(f32), axis=0) for item in query_parts + value_low]
    )
    dinput = (
        (dresid + normalize_back(dnorm_one, unit_one, inverse_one, gain_one))
        .astype(bf16)
        .reshape(images, slots, features)
    )

    pieces = [
        grad_gain_one,
        grad_shift_one,
        grad_qkv_bias.reshape(2, heads, shards, -1).transpose(2, 0, 1, 3),
        grad_proj_bias,
        grad_scale_one,
        grad_gain_two,
        grad_shift_two,
        grad_up_bias.reshape(up_bias.shape[0], shards, -1).transpose(1, 0, 2),
        grad_down_bias,
        grad_scale_two,
    ]
    sent_small = jnp.concatenate([item.reshape(shards, -1) for item in pieces], axis=1)
    got = lax.all_to_all(sent_small.astype(bf16), "fsdp", split_axis=0, concat_axis=0, tiled=True)
    total = jnp.sum(got.astype(f32), axis=0).astype(bf16)
    total = exchange_sum(total, "ctx")
    halves = sizes[0] + sizes[1]
    first_part = exchange_sum(total[:halves].astype(bf16), "tp")
    total = jnp.concatenate([first_part, total[halves:]])
    results = []
    offset = 0
    for item, size in zip(small, sizes):
        results.append(total[offset : offset + size].reshape(item.shape))
        offset += size
    (
        out_gain_one,
        out_shift_one,
        out_qkv_bias,
        out_proj_bias,
        out_scale_one,
        out_gain_two,
        out_shift_two,
        out_up_bias,
        out_down_bias,
        out_scale_two,
    ) = results
    return (
        output,
        dinput,
        out_gain_one,
        out_shift_one,
        jnp.stack([grad_qkv[:, i * width : (i + 1) * width] for i in range(3)], axis=1),
        out_qkv_bias,
        grad_proj,
        out_proj_bias,
        out_scale_one,
        out_gain_two,
        out_shift_two,
        grad_up,
        out_up_bias,
        grad_down,
        out_down_bias,
        out_scale_two,
    )


def solution(mesh):
    rows = P("fsdp", "ctx", None)
    vector = P("fsdp")
    params = (
        vector,
        vector,
        P("fsdp", None, "tp"),
        P(None, "tp", "fsdp"),
        P("tp", "fsdp"),
        vector,
        vector,
        vector,
        vector,
        P("fsdp", "tp"),
        P("tp", "fsdp"),
        P("tp", "fsdp"),
        vector,
        vector,
    )

    return jax.shard_map(
        body,
        mesh=mesh,
        in_specs=(rows, P("fsdp", None)) + params + (rows,),
        out_specs=(rows, rows) + params,
        check_vma=False,
    )
```
